512 devices in a mesh: chan: 8 (over z), sx: 8 (over x, core), sy: 8 (over y).
Axes of the slice: x: 4, y: 8, z: 8, core: 2. Of those that a mesh axis runs over, the one named last changes fastest.
Arguments:
- volume: bfloat16 [8, 64, 64, 256], P('sx', 'sy', None, 'chan'), may hold values from -6 to 6
- kernel: bfloat16 [27, 256, 256], P(None, 'chan'), may hold values from -0.078125 to 0.078125
- grad_out: bfloat16 [8, 64, 64, 256], P('sx', 'sy', None, 'chan'), may hold values from -6 to 6
Outputs:
- out: bfloat16 [8, 64, 64, 256], P('sx', 'sy', None, 'chan')
- grad_input: bfloat16 [8, 64, 64, 256], P('sx', 'sy', None, 'chan')
- grad_kernel: float32 [27, 256, 256], P(None, 'chan')
The draws below stay inside these ranges and needn't reach their ends.
All inputs are finite; a program needn't handle non-finite values.
Results may differ from the reference program's by a relative error of at most 0.0015.
Values may be sent and summed in bfloat16 or wider, within the bound.
No kernel may reach another device: no remote copies, remote signals or barrier semaphores. Data moves between devices by JAX's collectives and lax.ppermute only.
A program may use at most 64 MiB of HBM per device.

```python
import math
import jax
import jax.numpy as jnp

CIN = 256
COUT = 256
NX = 8
NY = 64
NZ = 64


def block_levels(stream_key, shape, cuts, least, largest):
    loudness = 1.0
    for axis_at, blocks in cuts:
        heights = jax.random.uniform(jax.random.fold_in(jax.random.fold_in(stream_key, 6), axis_at), (blocks,), jnp.float32, least / len(cuts), largest / len(cuts))
        loudness = loudness * jnp.repeat(jnp.exp(heights), shape[axis_at] // blocks).reshape((-1,) + (1,) * (len(shape) - 1 - axis_at))
    return loudness


def bell_draw(rng, dims, width, limit, shards=(), dtype=jnp.bfloat16):
    loudness = block_levels(rng, dims, shards, -0.22, 0.18) if shards else 1.0
    values = jax.random.normal(rng, dims, jnp.float32) * width * loudness
    return jnp.minimum(jnp.maximum(values, -limit), limit).astype(dtype)


def setup_inputs(seed: int = 0) -> dict:
    key_of = jax.random.split(jax.random.key(seed), 4)
    return {
        "volume": bell_draw(key_of[0], (NX, NY, NZ, CIN), 1.0, 6.0, ((0, 8), (1, 8), (3, 8))),
        "kernel": bell_draw(key_of[1], (27, CIN, COUT), (27 * CIN) ** -0.5, 0.078125, ((1, 8),)),
        "grad_out": bell_draw(key_of[2], (NX, NY, NZ, COUT), 1.0, 6.0, ((0, 8), (1, 8), (3, 8))),
    }


def reference(volume, kernel, grad_out):
    padded = jnp.pad(volume, ((1, 1), (1, 1), (1, 1), (0, 0)))
    grad_pad = jnp.pad(grad_out, ((1, 1), (1, 1), (1, 1), (0, 0)))
    flat_grad = grad_out.reshape(-1, COUT)
    result = jnp.zeros((NX * NY * NZ, COUT), jnp.float32)
    back = jnp.zeros((NX * NY * NZ, CIN), jnp.float32)
    kernel_terms = []
    for index in range(27):
        first, second, third = (index // 9, index // 3 % 3, index % 3)
        window = padded[first:first + NX, second:second + NY, third:third + NZ].reshape(-1, CIN)
        result = result + jnp.dot(window, kernel[index], preferred_element_type=jnp.float32)
        grad_win = grad_pad[2 - first:2 - first + NX, 2 - second:2 - second + NY, 2 - third:2 - third + NZ].reshape(-1, COUT)
        back = back + jnp.dot(grad_win, kernel[index].T, preferred_element_type=jnp.float32)
        kernel_terms.append(jnp.dot(window.T, flat_grad, preferred_element_type=jnp.float32))
    out = result.reshape(NX, NY, NZ, COUT).astype(jnp.bfloat16)
    grad_input = back.reshape(NX, NY, NZ, CIN).astype(jnp.bfloat16)
    grad_kernel = jnp.stack(kernel_terms) / jnp.float32(math.sqrt(NX * NY * NZ))
    return (out, grad_input, grad_kernel)
```

```python
import math

import jax
import jax.numpy as jnp
from jax import lax
from jax.experimental import pallas as pl
from jax.experimental.pallas import tpu as pltpu
from jax.sharding import Mesh
from jax.sharding import PartitionSpec as P

F32 = jnp.float32
BF16 = jnp.bfloat16
PLANE = ("x", "core")
PARAMS = pltpu.CompilerParams(vmem_limit_bytes=16 * 2**20)


def call(kernel, outs, flops, *args):
    moved = sum(a.size * a.dtype.itemsize for a in args)
    moved += sum(math.prod(s) * jnp.dtype(d).itemsize for s, d in outs)
    specs = [
        pl.BlockSpec(memory_space=pltpu.SMEM if a.dtype == jnp.int32 else pltpu.VMEM) for a in args
    ]
    return pl.pallas_call(
        kernel,
        out_shape=[jax.ShapeDtypeStruct(s, d) for s, d in outs],
        in_specs=specs,
        out_specs=[pl.BlockSpec(memory_space=pltpu.VMEM) for _ in outs],
        compiler_params=PARAMS,
        cost_estimate=pl.CostEstimate(flops=flops, bytes_accessed=moved, transcendentals=0),
    )(*args)


def edge_rows(v, g, first, last):
    c, rows = v.shape[1], v.shape[0]
    first[:c] = v[0]
    first[c:] = g[0]
    last[:c] = v[rows - 1]
    last[c:] = g[rows - 1]


def ring_rows(v, g, before, after, v_ring, g_copies):
    rows, c, z = v.shape
    for own, lo, out in ((v, 0, v_ring), (g, c, None)):
        parts = [own[r] for r in range(rows)]
        parts += [after[lo : lo + c], before[lo : lo + c]]
        ring = jnp.concatenate([part.astype(F32) for part in parts], axis=1).astype(BF16)
        if out is None:
            for copy in range(g_copies.shape[0]):
                g_copies[copy] = ring
        else:
            out[...] = ring


def in_line(shape, z, shift):
    at = lax.broadcasted_iota(jnp.int32, shape, 1) % z + shift
    return (at >= 0) & (at < z)


def forward_and_weights(z, core, below, own, above, g, k, keep, send, partial, columns):
    c = own.shape[0]
    lanes = own.shape[1]
    cells = lanes - 2 * z
    planes = jnp.concatenate([below[...], own[...], above[...]], axis=0).astype(F32)
    for e in range(3):
        moved = planes if e == 1 else pltpu.roll(planes, (1 - e) % lanes, 1)
        if e != 1:
            moved = jnp.where(in_line(moved.shape, z, e - 1), moved, 0.0)
        for b in range(3):
            window = moved if b == 1 else pltpu.roll(moved, (z * (1 - b)) % lanes, 1)
            window = window[:, :cells].astype(BF16)
            for a in range(3):
                at = (9 * a + 3 * b + e) * c
                columns[at : at + c, :] = window[a * c : (a + 1) * c]
    groups, total = g.shape[0], g.shape[0] * g.shape[1]
    g_own = g[...].reshape(total, lanes)[:, :cells]
    terms = lax.dot_general(
        columns[...], g_own, (((1,), (1,)), ((), ())), preferred_element_type=F32
    )
    half = total // 2
    low, high = terms[:, :half], terms[:, half:]
    first = core[0] == 0
    kept = jnp.where(first, low, high)
    sent = jnp.where(first, high, low)
    pieces, rows = keep.shape[0], keep.shape[1]
    for piece in range(pieces):
        keep[piece] = kept[piece * rows : (piece + 1) * rows]
        send[piece] = sent[piece * rows : (piece + 1) * rows]
    out = lax.dot_general(k[...], columns[...], (((0,), (0,)), ((), ())), preferred_element_type=F32)
    partial[...] = out.reshape(groups, total // groups, cells)


def input_gradient(z, below, own, above, k, out):
    rows, c = out.shape[0], out.shape[1]
    total = own.shape[0] * own.shape[1]
    lanes = own.shape[2]
    taps = k.shape[0] // 3
    terms = jnp.zeros((taps, lanes), F32)
    for a, plane in enumerate((above, own, below)):
        terms += jnp.dot(
            k[a * taps : (a + 1) * taps, :],
            plane[...].reshape(total, lanes),
            preferred_element_type=F32,
        )
    result = jnp.zeros((c, lanes), F32)
    for e in range(3):
        line = jnp.zeros((c, lanes), F32)
        for b in range(3):
            at = (3 * b + e) * c
            term = terms[at : at + c]
            line += term if b == 1 else pltpu.roll(term, (z * (b - 1)) % lanes, 1)
        if e != 1:
            line = pltpu.roll(line, (e - 1) % lanes, 1)
            line = jnp.where(in_line(line.shape, z, 1 - e), line, 0.0)
        result += line
    split_rows(result, out)


def split_rows(value, out):
    rows, z = out.shape[0], out.shape[2]
    lanes = value.shape[1]
    for r in range(rows):
        shifted = value if r == 0 else pltpu.roll(value, lanes - r * z, 1)
        out[r] = shifted[:, :z].astype(BF16)


def sum_outputs(partial, out):
    total = partial[0]
    for part in range(1, partial.shape[0]):
        total += partial[part]
    split_rows(total, out)


def add_halves(keep, other, out):
    out[...] = keep[...] + other[...]


def sum_pieces(scale, parts, out):
    total = parts[0]
    for part in range(1, parts.shape[0]):
        total += parts[part]
    total = total / scale
    for copy in range(out.shape[0]):
        out[copy] = total


def join_halves(core, mine, other, out):
    pieces, rows, half = mine.shape
    first = core[0] == 0
    for piece in range(pieces):
        a, b = mine[piece], other[piece]
        out[piece * rows : (piece + 1) * rows, :half] = jnp.where(first, a, b)
        out[piece * rows : (piece + 1) * rows, half:] = jnp.where(first, b, a)


def neighbours(value_up, value_down, axis):
    n = lax.axis_size(axis)
    up = [(i, i + 1) for i in range(n - 1)]
    down = [(i + 1, i) for i in range(n - 1)]
    return lax.ppermute(value_up, axis, up), lax.ppermute(value_down, axis, down)


def exchange(value, axis):
    return lax.all_to_all(value, axis, 0, 0, tiled=True)


def body(volume, kernel, grad_out):
    _, rows, z, c = volume.shape
    taps, _, total = kernel.shape
    cells, lanes = rows * z, (rows + 2) * z
    groups = lax.axis_size("chan")
    pieces = lax.axis_size("x") * lax.axis_size("sy")
    devices = pieces * lax.axis_size("core")
    v = volume[0].transpose(0, 2, 1)
    g = grad_out[0].transpose(0, 2, 1)
    k = kernel.reshape(taps * c, total)
    core = lax.axis_index("core").reshape(1)
    work = 2 * taps * c * total * cells

    first, last = call(edge_rows, [((2 * c, z), BF16)] * 2, 0, v, g)
    before, after = neighbours(last, first, "sy")
    v_ring, g_copies = call(
        ring_rows,
        [((c, lanes), BF16), ((groups, c, lanes), BF16)],
        0,
        v,
        g,
        before,
        after,
    )
    g_ring = exchange(g_copies, "chan")
    v_below, v_above = neighbours(v_ring, v_ring, PLANE)

    piece = (pieces, taps * c // pieces, total // 2)

    def weights(*refs):
        forward_and_weights(z, *refs)

    operands = (core, v_below, v_ring, v_above, g_ring, k)
    moved = sum(a.size * a.dtype.itemsize for a in operands) + 3 * math.prod(piece) * 4
    keep, send, partial = pl.pallas_call(
        weights,
        out_shape=[
            jax.ShapeDtypeStruct(piece, F32),
            jax.ShapeDtypeStruct(piece, F32),
            jax.ShapeDtypeStruct((groups, total // groups, cells), F32),
        ],
        in_specs=[pl.BlockSpec(memory_space=pltpu.SMEM)]
        + [pl.BlockSpec(memory_space=pltpu.VMEM)] * 5,
        out_specs=[pl.BlockSpec(memory_space=pltpu.VMEM)] * 3,
        scratch_shapes=[pltpu.VMEM((taps * c, cells), BF16)],
        compiler_params=PARAMS,
        cost_estimate=pl.CostEstimate(flops=2 * work, bytes_accessed=moved, transcendentals=0),
    )(*operands)

    swap = [(0, 1), (1, 0)]
    (halves,) = call(add_halves, [(piece, F32)], 0, keep, lax.ppermute(send, "core", swap))
    parts = exchange(halves, ("x", "sy"))
    scale = math.sqrt(cells * devices)

    def reduce_pieces(*refs):
        sum_pieces(scale, *refs)

    (copies,) = call(reduce_pieces, [(piece, F32)], 0, parts)
    mine = exchange(copies, ("x", "sy"))
    other = lax.ppermute(mine, "core", swap)
    (grad_kernel,) = call(join_halves, [((taps * c, total), F32)], 0, core, mine, other)

    (out,) = call(sum_outputs, [((rows, c, z), BF16)], 0, exchange(partial, "chan"))

    g_below, g_above = neighbours(g_ring, g_ring, PLANE)

    def inputs(*refs):
        input_gradient(z, *refs)

    (grad_input,) = call(inputs, [((rows, c, z), BF16)], work, g_below, g_ring, g_above, k)
    return (
        out.transpose(0, 2, 1)[None],
        grad_input.transpose(0, 2, 1)[None],
        grad_kernel.reshape(taps, c, total),
    )


def solution(mesh):
    cores = 2
    shape = (mesh.shape["chan"], mesh.shape["sx"] // cores, cores, mesh.shape["sy"])
    split = Mesh(mesh.devices.reshape(shape), ("chan", "x", "core", "sy"))
    cells = P(PLANE, "sy", None, "chan")
    weights = P(None, "chan", None)
    return jax.shard_map(
        body,
        mesh=split,
        in_specs=(cells, weights, cells),
        out_specs=(cells, cells, weights),
        check_vma=False,
    )
```

```python
import math

import jax
import jax.numpy as jnp
from jax import lax
from jax.experimental import pallas as pl
from jax.experimental.pallas import tpu as pltpu
from jax.sharding import Mesh
from jax.sharding import PartitionSpec as P

F32 = jnp.float32
BF16 = jnp.bfloat16
PLANE = ("x", "core")
PARAMS = pltpu.CompilerParams(vmem_limit_bytes=16 * 2**20)


def call(kernel, outs, flops, *args):
    moved = sum(a.size * a.dtype.itemsize for a in args)
    moved += sum(math.prod(s) * jnp.dtype(d).itemsize for s, d in outs)
    specs = [
        pl.BlockSpec(memory_space=pltpu.SMEM if a.dtype == jnp.int32 else pltpu.VMEM) for a in args
    ]
    return pl.pallas_call(
        kernel,
        out_shape=[jax.ShapeDtypeStruct(s, d) for s, d in outs],
        in_specs=specs,
        out_specs=[pl.BlockSpec(memory_space=pltpu.VMEM) for _ in outs],
        compiler_params=PARAMS,
        cost_estimate=pl.CostEstimate(flops=flops, bytes_accessed=moved, transcendentals=0),
    )(*args)


def edge_rows(v, g, first, last, sems):
    rows, c = v.shape[0], v.shape[1]
    copies = []
    for row, out in ((0, first), (rows - 1, last)):
        for i, source in enumerate((v, g)):
            to = out.at[pl.ds(i * c, c)]
            copies.append(pltpu.make_async_copy(source.at[row], to, sems.at[len(copies)]))
    for copy in copies:
        copy.start()
    for copy in copies:
        copy.wait()


def ring_rows(v, g, before, after, v_ring, g_copies):
    rows, c, z = v.shape
    for own, lo, out in ((v, 0, v_ring), (g, c, None)):
        parts = [own[r] for r in range(rows)]
        parts += [after[lo : lo + c], before[lo : lo + c]]
        ring = jnp.concatenate([part.astype(F32) for part in parts], axis=1).astype(BF16)
        if out is None:
            for copy in range(g_copies.shape[0]):
                g_copies[copy] = ring
        else:
            out[...] = ring


def in_line(shape, z, shift):
    at = lax.broadcasted_iota(jnp.int32, shape, 1) % z + shift
    return (at >= 0) & (at < z)


def forward_and_weights(z, at_device, below, own, above, g, k, keep, send, o_keep, o_send, columns):
    c = own.shape[0]
    lanes = own.shape[1]
    cells = lanes - 2 * z
    planes = jnp.concatenate([below[...], own[...], above[...]], axis=0).astype(F32)
    for e in range(3):
        moved = planes if e == 1 else pltpu.roll(planes, (1 - e) % lanes, 1)
        if e != 1:
            moved = jnp.where(in_line(moved.shape, z, e - 1), moved, 0.0)
        for b in range(3):
            window = moved if b == 1 else pltpu.roll(moved, (z * (1 - b)) % lanes, 1)
            window = window[:, :cells].astype(BF16)
            for a in range(3):
                at = (9 * a + 3 * b + e) * c
                columns[at : at + c, :] = window[a * c : (a + 1) * c]
    groups, total = g.shape[0], g.shape[0] * g.shape[1]
    g_own = g[...].reshape(total, lanes)[:, :cells]
    terms = lax.dot_general(
        columns[...], g_own, (((1,), (1,)), ((), ())), preferred_element_type=F32
    )
    half = total // 2
    low, high = terms[:, :half], terms[:, half:]
    first = at_device[0] == 0
    kept = jnp.where(first, low, high)
    sent = jnp.where(first, high, low)
    pieces, rows = keep.shape[0], keep.shape[1]
    for piece in range(pieces):
        keep[piece] = kept[piece * rows : (piece + 1) * rows]
        send[piece] = sent[piece * rows : (piece + 1) * rows]
    out = lax.dot_general(k[...], columns[...], (((0,), (0,)), ((), ())), preferred_element_type=F32)
    out = out.reshape(groups // 2, 2, total // groups, cells)
    even = at_device[1] % 2 == 0
    o_keep[...] = jnp.where(even, out[:, 0], out[:, 1])
    o_send[...] = jnp.where(even, out[:, 1], out[:, 0])


def halve_outputs(bit, at_device, mine, other, o_keep, o_send):
    even = (at_device[1] // bit) % 2 == 0
    for i in range(o_keep.shape[0]):
        a = mine[2 * i] + other[2 * i]
        b = mine[2 * i + 1] + other[2 * i + 1]
        o_keep[i] = jnp.where(even, a, b)
        o_send[i] = jnp.where(even, b, a)


def input_gradient(z, below, own, above, k, out):
    rows, c = out.shape[0], out.shape[1]
    total = own.shape[0] * own.shape[1]
    lanes = own.shape[2]
    taps = k.shape[0] // 3
    terms = jnp.zeros((taps, lanes), F32)
    for a, plane in enumerate((above, own, below)):
        terms += jnp.dot(
            k[a * taps : (a + 1) * taps, :],
            plane[...].reshape(total, lanes),
            preferred_element_type=F32,
        )
    result = jnp.zeros((c, lanes), F32)
    for e in range(3):
        line = jnp.zeros((c, lanes), F32)
        for b in range(3):
            at = (3 * b + e) * c
            term = terms[at : at + c]
            line += term if b == 1 else pltpu.roll(term, (z * (b - 1)) % lanes, 1)
        if e != 1:
            line = pltpu.roll(line, (e - 1) % lanes, 1)
            line = jnp.where(in_line(line.shape, z, 1 - e), line, 0.0)
        result += line
    split_rows(result, out)


def split_rows(value, out):
    rows, z = out.shape[0], out.shape[2]
    lanes = value.shape[1]
    for r in range(rows):
        shifted = value if r == 0 else pltpu.roll(value, lanes - r * z, 1)
        out[r] = shifted[:, :z].astype(BF16)


def sum_outputs(mine, other, out):
    split_rows(mine[0] + other[0], out)


def add_halves(keep, other, out):
    out[...] = keep[...] + other[...]


def sum_pieces(scale, parts, out):
    total = parts[0]
    for part in range(1, parts.shape[0]):
        total += parts[part]
    total = total / scale
    for copy in range(out.shape[0]):
        out[copy] = total


def join_halves(at_device, mine, other, out):
    pieces, rows, half = mine.shape
    first = at_device[0] == 0
    for piece in range(pieces):
        a, b = mine[piece], other[piece]
        out[piece * rows : (piece + 1) * rows, :half] = jnp.where(first, a, b)
        out[piece * rows : (piece + 1) * rows, half:] = jnp.where(first, b, a)


def neighbours(value_up, value_down, axis):
    n = lax.axis_size(axis)
    up = [(i, i + 1) for i in range(n - 1)]
    down = [(i + 1, i) for i in range(n - 1)]
    return lax.ppermute(value_up, axis, up), lax.ppermute(value_down, axis, down)


def swapped(value, bit):
    return lax.ppermute(value, "chan", [(i, i ^ bit) for i in range(lax.axis_size("chan"))])


def exchange(value, axis):
    return lax.all_to_all(value, axis, 0, 0, tiled=True)


def body(volume, kernel, grad_out):
    _, rows, z, c = volume.shape
    taps, _, total = kernel.shape
    cells, lanes = rows * z, (rows + 2) * z
    groups = lax.axis_size("chan")
    pieces = lax.axis_size("x") * lax.axis_size("sy")
    devices = pieces * lax.axis_size("core")
    v = volume[0].transpose(0, 2, 1)
    g = grad_out[0].transpose(0, 2, 1)
    k = kernel.reshape(taps * c, total)
    at_device = jnp.stack([lax.axis_index("core"), lax.axis_index("chan")]).astype(jnp.int32)
    work = 2 * taps * c * total * cells

    edge = jax.ShapeDtypeStruct((2 * c, z), BF16)
    first, last = pl.pallas_call(
        edge_rows,
        out_shape=[edge, edge],
        in_specs=[pl.BlockSpec(memory_space=pltpu.HBM)] * 2,
        out_specs=[pl.BlockSpec(memory_space=pltpu.VMEM)] * 2,
        scratch_shapes=[pltpu.SemaphoreType.DMA((4,))],
        compiler_params=PARAMS,
        cost_estimate=pl.CostEstimate(flops=0, bytes_accessed=4 * c * z * 2, transcendentals=0),
    )(v, g)
    before, after = neighbours(last, first, "sy")
    v_ring, g_copies = call(
        ring_rows,
        [((c, lanes), BF16), ((groups, c, lanes), BF16)],
        0,
        v,
        g,
        before,
        after,
    )
    g_ring = exchange(g_copies, "chan")
    v_below, v_above = neighbours(v_ring, v_ring, PLANE)

    piece = (pieces, taps * c // pieces, total // 2)

    def weights(*refs):
        forward_and_weights(z, *refs)

    operands = (at_device, v_below, v_ring, v_above, g_ring, k)
    moved = sum(a.size * a.dtype.itemsize for a in operands) + 3 * math.prod(piece) * 4
    block = (total // groups, cells)
    keep, send, o_keep, o_send = pl.pallas_call(
        weights,
        out_shape=[jax.ShapeDtypeStruct(piece, F32)] * 2
        + [jax.ShapeDtypeStruct((groups // 2, *block), F32)] * 2,
        in_specs=[pl.BlockSpec(memory_space=pltpu.SMEM)]
        + [pl.BlockSpec(memory_space=pltpu.VMEM)] * 5,
        out_specs=[pl.BlockSpec(memory_space=pltpu.VMEM)] * 4,
        scratch_shapes=[pltpu.VMEM((taps * c, cells), BF16)],
        compiler_params=PARAMS,
        cost_estimate=pl.CostEstimate(flops=2 * work, bytes_accessed=moved, transcendentals=0),
    )(*operands)

    swap = [(0, 1), (1, 0)]
    (halves,) = call(add_halves, [(piece, F32)], 0, keep, lax.ppermute(send, "core", swap))
    halves, o_send, g_ring = lax.optimization_barrier((halves, o_send, g_ring))
    parts = exchange(halves, ("x", "sy"))
    g_below, g_above = neighbours(g_ring, g_ring, PLANE)
    bit = 1
    o_other = swapped(o_send, bit)
    parts, o_other, g_below, g_above = lax.optimization_barrier((parts, o_other, g_below, g_above))
    scale = math.sqrt(cells * devices)

    def reduce_pieces(*refs):
        sum_pieces(scale, *refs)

    (copies,) = call(reduce_pieces, [(piece, F32)], 0, parts)
    copies, o_other = lax.optimization_barrier((copies, o_other))
    mine = exchange(copies, ("x", "sy"))

    while o_keep.shape[0] > 1:
        bit *= 2

        def halve(*refs, bit=bit):
            halve_outputs(bit, *refs)

        left = [((o_keep.shape[0] // 2, *block), F32)] * 2
        o_keep, o_send = call(halve, left, 0, at_device, o_keep, o_other)
        o_other = swapped(o_send, bit)
    (out,) = call(sum_outputs, [((rows, c, z), BF16)], 0, o_keep, o_other)

    def inputs(*refs):
        input_gradient(z, *refs)

    (grad_input,) = call(inputs, [((rows, c, z), BF16)], work, g_below, g_ring, g_above, k)
    mine, out, grad_input = lax.optimization_barrier((mine, out, grad_input))
    other = lax.ppermute(mine, "core", swap)
    (grad_kernel,) = call(join_halves, [((taps * c, total), F32)], 0, at_device, mine, other)
    return (
        out.transpose(0, 2, 1)[None],
        grad_input.transpose(0, 2, 1)[None],
        grad_kernel.reshape(taps, c, total),
    )


def solution(mesh):
    cores = 2
    shape = (mesh.shape["chan"], mesh.shape["sx"] // cores, cores, mesh.shape["sy"])
    split = Mesh(mesh.devices.reshape(shape), ("chan", "x", "core", "sy"))
    cells = P(PLANE, "sy", None, "chan")
    weights = P(None, "chan", None)
    return jax.shard_map(
        body,
        mesh=split,
        in_specs=(cells, weights, cells),
        out_specs=(cells, cells, weights),
        check_vma=False,
    )
```

```python
import math

import jax
import jax.numpy as jnp
from jax import lax
from jax.experimental import pallas as pl
from jax.experimental.pallas import tpu as pltpu
from jax.sharding import Mesh
from jax.sharding import PartitionSpec as P

F32 = jnp.float32
BF16 = jnp.bfloat16
PLANE = ("x", "core")
PARAMS = pltpu.CompilerParams(vmem_limit_bytes=16 * 2**20)


def call(kernel, outs, flops, *args):
    moved = sum(a.size * a.dtype.itemsize for a in args)
    moved += sum(math.prod(s) * jnp.dtype(d).itemsize for s, d in outs)
    specs = [
        pl.BlockSpec(memory_space=pltpu.SMEM if a.dtype == jnp.int32 else pltpu.VMEM) for a in args
    ]
    return pl.pallas_call(
        kernel,
        out_shape=[jax.ShapeDtypeStruct(s, d) for s, d in outs],
        in_specs=specs,
        out_specs=[pl.BlockSpec(memory_space=pltpu.VMEM) for _ in outs],
        compiler_params=PARAMS,
        cost_estimate=pl.CostEstimate(flops=flops, bytes_accessed=moved, transcendentals=0),
    )(*args)


def first_sends(v, g, k, first, last, sends, v_own, g_own, k_own, sems):
    rows, c, z = g_own.shape
    cells, weights = rows * z, k.shape[0]
    moves = [
        pltpu.make_async_copy(v, v_own, sems.at[0]),
        pltpu.make_async_copy(g, g_own, sems.at[1]),
        pltpu.make_async_copy(k, k_own.at[pl.ds(0, weights)], sems.at[2]),
    ]
    for move in moves:
        move.start()
    k_own[weights:] = jnp.zeros((k_own.shape[0] - weights, k_own.shape[1]), BF16)
    moves[0].wait()
    first[...] = v_own[0]
    last[...] = v_own[rows - 1]
    v_flat = in_row([v_own[r] for r in range(rows)])
    moves[1].wait()
    g_flat = in_row([g_own[r] for r in range(rows)])
    moves[2].wait()
    turned = k_own[...].astype(F32).T.astype(BF16)
    for to in range(sends.shape[0]):
        sends[to, :, :cells] = g_flat
        sends[to, :, cells : 2 * cells] = v_flat
        sends[to, :, 2 * cells :] = turned[to * c : (to + 1) * c]


def in_row(parts):
    return jnp.concatenate([part.astype(F32) for part in parts], axis=1).astype(BF16)


def volume_ring(v, before, after, ring):
    ring[...] = in_row([v[r] for r in range(v.shape[0])] + [after[...], before[...]])


def both_rings(received, before, after, ring):
    groups, c, _ = received.shape
    half, z = groups * c, before.shape[1]
    cells = ring.shape[1] - 2 * z
    ring[:half, :cells] = received[:, :, :cells].reshape(half, cells)
    ring[half:, :cells] = received[:, :, cells : 2 * cells].reshape(half, cells)
    ring[:, cells:] = in_row([after[...], before[...]])


def weights_by_output(received, k_out):
    groups, c, width = received.shape
    taps = k_out.shape[0] // c
    start = width - pl.cdiv(taps * c, 128) * 128
    for tap in range(taps):
        at = start + tap * c
        k_out[tap * c : (tap + 1) * c] = in_row([received[i][:, at : at + c] for i in range(groups)])


def in_line(shape, z, shift):
    at = lax.broadcasted_iota(jnp.int32, shape, 1) % z + shift
    return (at >= 0) & (at < z)


def windows(z, below, own, above, columns):
    c = own.shape[0]
    lanes = own.shape[1]
    cells = lanes - 2 * z
    planes = jnp.concatenate([below[...], own[...], above[...]], axis=0).astype(F32)
    for e in range(3):
        moved = planes if e == 1 else pltpu.roll(planes, (1 - e) % lanes, 1)
        if e != 1:
            moved = jnp.where(in_line(moved.shape, z, e - 1), moved, 0.0)
        for b in range(3):
            window = moved if b == 1 else pltpu.roll(moved, (z * (1 - b)) % lanes, 1)
            window = window[:, :cells].astype(BF16)
            for a in range(3):
                at = (9 * a + 3 * b + e) * c
                columns[at : at + c, :] = window[a * c : (a + 1) * c]


def weight_terms(core, columns, received, keep, send, first, last):
    groups, c, _ = received.shape
    cells, total, z = columns.shape[1], groups * c, first.shape[1]
    g_own = received[:, :, :cells].reshape(total, cells)
    terms = lax.dot_general(
        columns[...], g_own, (((1,), (1,)), ((), ())), preferred_element_type=F32
    )
    half = total // 2
    low, high = terms[:, :half], terms[:, half:]
    is_low = core[0] == 0
    kept = jnp.where(is_low, low, high)
    sent = jnp.where(is_low, high, low)
    pieces, rows = keep.shape[0], keep.shape[1]
    for piece in range(pieces):
        keep[piece] = kept[piece * rows : (piece + 1) * rows]
        send[piece] = sent[piece * rows : (piece + 1) * rows]
    for i in range(2):
        at = slice(i * total, (i + 1) * total)
        first[at] = received[:, :, i * cells : i * cells + z].reshape(total, z)
        end = received[:, :, (i + 1) * cells - 2 * z : (i + 1) * cells].reshape(total, 2 * z)
        last[at] = pltpu.roll(end.astype(F32), z, 1)[:, :z].astype(BF16)


def convolve(z, sign, planes, k, out):
    lanes = planes[0].shape[1]
    taps = k.shape[0] // 3
    c = taps // 9
    terms = jnp.zeros((taps, lanes), F32)
    for a, plane in enumerate(planes[::sign]):
        terms += jnp.dot(k[a * taps : (a + 1) * taps, :], plane, preferred_element_type=F32)
    result = jnp.zeros((c, lanes), F32)
    for e in range(3):
        line = jnp.zeros((c, lanes), F32)
        for b in range(3):
            at = (3 * b + e) * c
            term = terms[at : at + c]
            line += term if b == 1 else pltpu.roll(term, (sign * z * (1 - b)) % lanes, 1)
        if e != 1:
            line = pltpu.roll(line, (sign * (1 - e)) % lanes, 1)
            line = jnp.where(in_line(line.shape, z, sign * (e - 1)), line, 0.0)
        result += line
    split_rows(result, out)


def both_convolutions(z, below, own, above, k, k_out, out, grad_input):
    half = own.shape[0] // 2
    convolve(z, 1, [ref[half:] for ref in (below, own, above)], k_out, out)
    convolve(z, -1, [ref[:half] for ref in (below, own, above)], k, grad_input)


def split_rows(value, out):
    rows, z = out.shape[0], out.shape[2]
    lanes = value.shape[1]
    for r in range(rows):
        shifted = value if r == 0 else pltpu.roll(value, lanes - r * z, 1)
        out[r] = shifted[:, :z].astype(BF16)


def add_halves(keep, other, out):
    out[...] = keep[...] + other[...]


def sum_pieces(scale, parts, out):
    total = parts[0]
    for part in range(1, parts.shape[0]):
        total += parts[part]
    total = total / scale
    for copy in range(out.shape[0]):
        out[copy] = total


def join_halves(core, mine, other, out):
    pieces, rows, half = mine.shape
    first = core[0] == 0
    for piece in range(pieces):
        a, b = mine[piece], other[piece]
        out[piece * rows : (piece + 1) * rows, :half] = jnp.where(first, a, b)
        out[piece * rows : (piece + 1) * rows, half:] = jnp.where(first, b, a)


def neighbours(value_up, value_down, axis):
    n = lax.axis_size(axis)
    up = [(i, i + 1) for i in range(n - 1)]
    down = [(i + 1, i) for i in range(n - 1)]
    return lax.ppermute(value_up, axis, up), lax.ppermute(value_down, axis, down)


def exchange(value, axis):
    return lax.all_to_all(value, axis, 0, 0, tiled=True)


def body(volume, kernel, grad_out):
    _, rows, z, c = volume.shape
    taps, _, total = kernel.shape
    cells, lanes = rows * z, (rows + 2) * z
    groups = lax.axis_size("chan")
    pieces = lax.axis_size("x") * lax.axis_size("sy")
    devices = pieces * lax.axis_size("core")
    v = volume[0].transpose(0, 2, 1)
    g = grad_out[0].transpose(0, 2, 1)
    k = kernel.reshape(taps * c, total)
    core = lax.axis_index("core").reshape(1).astype(jnp.int32)
    work = 2 * taps * c * total * cells
    weights = pl.cdiv(taps * c, 128) * 128
    width = 2 * cells + weights

    edge = jax.ShapeDtypeStruct((c, z), BF16)
    first, last, sends = pl.pallas_call(
        first_sends,
        out_shape=[edge, edge, jax.ShapeDtypeStruct((groups, c, width), BF16)],
        in_specs=[pl.BlockSpec(memory_space=pltpu.HBM)] * 3,
        out_specs=[pl.BlockSpec(memory_space=pltpu.VMEM)] * 3,
        scratch_shapes=[
            pltpu.VMEM((rows, c, z), BF16),
            pltpu.VMEM((rows, c, z), BF16),
            pltpu.VMEM((weights, total), BF16),
            pltpu.SemaphoreType.DMA((3,)),
        ],
        compiler_params=pltpu.CompilerParams(vmem_limit_bytes=60 * 2**20),
        cost_estimate=pl.CostEstimate(
            flops=0, bytes_accessed=groups * c * width * 4, transcendentals=0
        ),
    )(v, g, k)
    before, after = neighbours(last, first, "sy")
    received = exchange(sends, "chan")
    (v_ring,) = call(volume_ring, [((c, lanes), BF16)], 0, v, before, after)
    v_below, v_above = neighbours(v_ring, v_ring, PLANE)

    def around(*refs):
        windows(z, *refs)

    (columns,) = call(around, [((taps * c, cells), BF16)], 0, v_below, v_ring, v_above)
    piece = (pieces, taps * c // pieces, total // 2)
    end = ((2 * total, z), BF16)
    keep, send, first, last = call(
        weight_terms, [(piece, F32), (piece, F32), end, end], work, core, columns, received
    )
    swap = [(0, 1), (1, 0)]
    (halves,) = call(add_halves, [(piece, F32)], 0, keep, lax.ppermute(send, "core", swap))

    halves, first, last, received = lax.optimization_barrier((halves, first, last, received))
    parts = exchange(halves, ("x", "sy"))
    before, after = neighbours(last, first, "sy")
    (ring,) = call(both_rings, [((2 * total, lanes), BF16)], 0, received, before, after)
    (k_out,) = call(weights_by_output, [((taps * c, total), BF16)], 0, received)
    parts, ring, k_out = lax.optimization_barrier((parts, ring, k_out))
    scale = math.sqrt(cells * devices)

    def reduce_pieces(*refs):
        sum_pieces(scale, *refs)

    (copies,) = call(reduce_pieces, [(piece, F32)], 0, parts)
    copies, ring = lax.optimization_barrier((copies, ring))
    mine = exchange(copies, ("x", "sy"))
    below, above = neighbours(ring, ring, PLANE)

    def convolutions(*refs):
        both_convolutions(z, *refs)

    result = ((rows, c, z), BF16)
    out, grad_input = call(convolutions, [result, result], 2 * work, below, ring, above, k, k_out)
    mine, out, grad_input = lax.optimization_barrier((mine, out, grad_input))
    other = lax.ppermute(mine, "core", swap)
    (grad_kernel,) = call(join_halves, [((taps * c, total), F32)], 0, core, mine, other)
    return (
        out.transpose(0, 2, 1)[None],
        grad_input.transpose(0, 2, 1)[None],
        grad_kernel.reshape(taps, c, total),
    )


def solution(mesh):
    cores = 2
    shape = (mesh.shape["chan"], mesh.shape["sx"] // cores, cores, mesh.shape["sy"])
    split = Mesh(mesh.devices.reshape(shape), ("chan", "x", "core", "sy"))
    cells = P(PLANE, "sy", None, "chan")
    weights = P(None, "chan", None)
    return jax.shard_map(
        body,
        mesh=split,
        in_specs=(cells, weights, cells),
        out_specs=(cells, cells, weights),
        check_vma=False,
    )
```

```python
import math

import jax
import jax.numpy as jnp
from jax import lax
from jax.experimental import pallas as pl
from jax.experimental.pallas import tpu as pltpu
from jax.sharding import Mesh
from jax.sharding import PartitionSpec as P

F32 = jnp.float32
BF16 = jnp.bfloat16
PLANE = ("x", "core")
TAPS = 27
PARAMS = pltpu.CompilerParams(vmem_limit_bytes=16 * 2**20)


def call(kernel, outs, flops, *args):
    moved = sum(a.size * a.dtype.itemsize for a in args)
    moved += sum(math.prod(s) * jnp.dtype(d).itemsize for s, d in outs)
    specs = [
        pl.BlockSpec(memory_space=pltpu.SMEM if a.dtype == jnp.int32 else pltpu.VMEM) for a in args
    ]
    return pl.pallas_call(
        kernel,
        out_shape=[jax.ShapeDtypeStruct(s, d) for s, d in outs],
        in_specs=specs,
        out_specs=[pl.BlockSpec(memory_space=pltpu.VMEM) for _ in outs],
        compiler_params=PARAMS,
        cost_estimate=pl.CostEstimate(flops=flops, bytes_accessed=moved, transcendentals=0),
    )(*args)


def first_sends(core, v, g, k, first, last, sends, v_own, g_own, k_own, sems):
    rows, c, z = g_own.shape
    cells, weights = rows * z, k.shape[0]
    moves = [
        pltpu.make_async_copy(v, v_own, sems.at[0]),
        pltpu.make_async_copy(g, g_own, sems.at[1]),
        pltpu.make_async_copy(k, k_own.at[pl.ds(0, weights)], sems.at[2]),
    ]
    for move in moves:
        move.start()
    k_own[weights:] = jnp.zeros((k_own.shape[0] - weights, k_own.shape[1]), BF16)
    moves[0].wait()
    first[...] = v_own[0]
    last[...] = v_own[rows - 1]
    v_flat = in_row([v_own[r] for r in range(rows)])
    moves[1].wait()
    g_flat = in_row([g_own[r] for r in range(rows)])
    moves[2].wait()
    turned = k_own[...].astype(F32).T
    width = sends.shape[2] - 2 * cells
    later = pltpu.roll(turned, k_own.shape[0] - (weights // c // 2) * c, 1)
    half = jnp.where(core[0] == 0, turned[:, :width], later[:, :width]).astype(BF16)
    for to in range(sends.shape[0]):
        sends[to, :, :cells] = g_flat
        sends[to, :, cells : 2 * cells] = v_flat
        sends[to, :, 2 * cells :] = half[to * c : (to + 1) * c]


def in_row(parts):
    return jnp.concatenate([part.astype(F32) for part in parts], axis=1).astype(BF16)


def volume_ring(v, before, after, ring):
    ring[...] = in_row([v[r] for r in range(v.shape[0])] + [after[...], before[...]])


def weights_by_output(core, mine, other, k_out):
    c = k_out.shape[0] // TAPS
    groups = mine.shape[0] // c
    middle = TAPS // 2
    is_low = core[0] == 0
    a, b = mine[...], other[...]
    for tap in range(TAPS):
        half = jnp.where(is_low, a, b) if tap < middle else jnp.where(is_low, b, a)
        at = (tap if tap < middle else tap - middle) * c
        blocks = [half[i * c : (i + 1) * c, at : at + c] for i in range(groups)]
        k_out[tap * c : (tap + 1) * c] = in_row(blocks)


def in_line(shape, z, shift):
    at = lax.broadcasted_iota(jnp.int32, shape, 1) % z + shift
    return (at >= 0) & (at < z)


def windows(z, below, own, above, columns):
    c = own.shape[0]
    lanes = own.shape[1]
    cells = lanes - 2 * z
    planes = jnp.concatenate([below[...], own[...], above[...]], axis=0).astype(F32)
    for e in range(3):
        moved = planes if e == 1 else pltpu.roll(planes, (1 - e) % lanes, 1)
        if e != 1:
            moved = jnp.where(in_line(moved.shape, z, e - 1), moved, 0.0)
        for b in range(3):
            window = moved if b == 1 else pltpu.roll(moved, (z * (1 - b)) % lanes, 1)
            window = window[:, :cells].astype(BF16)
            for a in range(3):
                at = (9 * a + 3 * b + e) * c
                columns[at : at + c, :] = window[a * c : (a + 1) * c]


def weight_terms(core, columns, received, keep, send, k_mine):
    groups, c, _ = received.shape
    cells, total = columns.shape[1], groups * c
    g_own = received[:, :, :cells].reshape(total, cells)
    terms = lax.dot_general(
        columns[...], g_own, (((1,), (1,)), ((), ())), preferred_element_type=F32
    )
    half = total // 2
    low, high = terms[:, :half], terms[:, half:]
    is_low = core[0] == 0
    kept = jnp.where(is_low, low, high)
    sent = jnp.where(is_low, high, low)
    pieces, rows = keep.shape[0], keep.shape[1]
    for piece in range(pieces):
        keep[piece] = kept[piece * rows : (piece + 1) * rows]
        send[piece] = sent[piece * rows : (piece + 1) * rows]
    k_mine[...] = received[:, :, 2 * cells : 2 * cells + k_mine.shape[1]].reshape(k_mine.shape)


def spread(z, sign, own, k):
    lanes = own.shape[1] + 2 * z
    taps = k.shape[0] // 3
    c = taps // 9
    result = []
    for a in range(3)[:: -sign]:
        terms = jnp.dot(k[a * taps : (a + 1) * taps, :], own, preferred_element_type=F32)
        terms = jnp.concatenate([terms, jnp.zeros((taps, 2 * z), F32)], axis=1)
        plane = jnp.zeros((c, lanes), F32)
        for e in range(3):
            line = jnp.zeros((c, lanes), F32)
            for b in range(3):
                at = (3 * b + e) * c
                term = terms[at : at + c]
                line += term if b == 1 else pltpu.roll(term, (sign * z * (1 - b)) % lanes, 1)
            if e != 1:
                line = pltpu.roll(line, (sign * (1 - e)) % lanes, 1)
                line = jnp.where(in_line(line.shape, z, sign * (e - 1)), line, 0.0)
            plane += line
        result.append(plane)
    return result


def store_spread(planes, middle, up, down):
    c, cells = middle.shape[0] // 3, middle.shape[1]
    z = up.shape[1]
    for i, plane in enumerate(planes):
        at = slice(i * c, (i + 1) * c)
        middle[at] = plane[:, :cells]
        ends = plane[:, cells:]
        up[at] = ends[:, :z]
        down[at] = pltpu.roll(ends, z, 1)[:, :z]


def spread_cotangent(z, received, k, middle, up, down):
    groups, c, _ = received.shape
    cells = middle.shape[1]
    own = received[:, :, :cells].reshape(groups * c, cells)
    store_spread(spread(z, -1, own, k), middle, up, down)


def spread_volume(z, received, k_out, g_up, g_down, middle, up, down):
    groups, c, _ = received.shape
    cells = middle.shape[1]
    own = received[:, :, cells : 2 * cells].reshape(groups * c, cells)
    rows = g_up.shape[0]
    store_spread(spread(z, 1, own, k_out), middle, up.at[pl.ds(rows, rows)], down.at[pl.ds(rows, rows)])
    up[:rows] = g_up[...]
    down[:rows] = g_down[...]


def add_ends(g_middle, v_middle, before, after, own, to_below, to_above):
    rows, cells = g_middle.shape
    z, c = before.shape[1], rows // 3
    first = jnp.concatenate([before[...], jnp.zeros((2 * rows, z), F32)], axis=1)
    last = jnp.concatenate([jnp.zeros((2 * rows, z), F32), after[...]], axis=1)
    for i, middle in enumerate((g_middle, v_middle)):
        for part, out in enumerate((to_below, own, to_above)):
            at = slice(part * c, (part + 1) * c)
            from_end = slice(i * rows + part * c, i * rows + (part + 1) * c)
            value = middle[at]
            to = slice(i * c, (i + 1) * c)
            out[to] = value
            out[to, : 2 * z] = value[:, : 2 * z] + first[from_end]
            out[to, cells - 2 * z :] = value[:, cells - 2 * z :] + last[from_end]


def add_planes(own, below, above, out, grad_input):
    total = own[...] + below[...] + above[...]
    c = total.shape[0] // 2
    split_rows(total[c:], out)
    split_rows(total[:c], grad_input)


def split_rows(value, out):
    rows, z = out.shape[0], out.shape[2]
    lanes = value.shape[1]
    for r in range(rows):
        shifted = value if r == 0 else pltpu.roll(value, lanes - r * z, 1)
        out[r] = shifted[:, :z].astype(BF16)


def add_halves(keep, other, out):
    out[...] = keep[...] + other[...]


def sum_pieces(scale, parts, out):
    total = parts[0]
    for part in range(1, parts.shape[0]):
        total += parts[part]
    total = total / scale
    for copy in range(out.shape[0]):
        out[copy] = total


def join_halves(core, mine, other, out):
    pieces, rows, half = mine.shape
    first = core[0] == 0
    for piece in range(pieces):
        a, b = mine[piece], other[piece]
        out[piece * rows : (piece + 1) * rows, :half] = jnp.where(first, a, b)
        out[piece * rows : (piece + 1) * rows, half:] = jnp.where(first, b, a)


def neighbours(value_up, value_down, axis):
    n = lax.axis_size(axis)
    up = [(i, i + 1) for i in range(n - 1)]
    down = [(i + 1, i) for i in range(n - 1)]
    return lax.ppermute(value_up, axis, up), lax.ppermute(value_down, axis, down)


def exchange(value, axis):
    return lax.all_to_all(value, axis, 0, 0, tiled=True)


def body(volume, kernel, grad_out):
    _, rows, z, c = volume.shape
    taps, _, total = kernel.shape
    cells, lanes = rows * z, (rows + 2) * z
    groups = lax.axis_size("chan")
    pieces = lax.axis_size("x") * lax.axis_size("sy")
    devices = pieces * lax.axis_size("core")
    v = volume[0].transpose(0, 2, 1)
    g = grad_out[0].transpose(0, 2, 1)
    k = kernel.reshape(taps * c, total)
    core = lax.axis_index("core").reshape(1).astype(jnp.int32)
    work = 2 * taps * c * total * cells
    weights = pl.cdiv(taps * c, 128) * 128
    half_taps = (taps - taps // 2) * c
    width = 2 * cells + pl.cdiv(half_taps, 128) * 128

    edge = jax.ShapeDtypeStruct((c, z), BF16)
    first, last, sends = pl.pallas_call(
        first_sends,
        out_shape=[edge, edge, jax.ShapeDtypeStruct((groups, c, width), BF16)],
        in_specs=[pl.BlockSpec(memory_space=pltpu.SMEM)]
        + [pl.BlockSpec(memory_space=pltpu.HBM)] * 3,
        out_specs=[pl.BlockSpec(memory_space=pltpu.VMEM)] * 3,
        scratch_shapes=[
            pltpu.VMEM((rows, c, z), BF16),
            pltpu.VMEM((rows, c, z), BF16),
            pltpu.VMEM((weights, total), BF16),
            pltpu.SemaphoreType.DMA((3,)),
        ],
        compiler_params=pltpu.CompilerParams(vmem_limit_bytes=60 * 2**20),
        cost_estimate=pl.CostEstimate(
            flops=0, bytes_accessed=groups * c * width * 4, transcendentals=0
        ),
    )(core, v, g, k)
    before, after = neighbours(last, first, "sy")
    received = exchange(sends, "chan")
    (v_ring,) = call(volume_ring, [((c, lanes), BF16)], 0, v, before, after)
    v_below, v_above = neighbours(v_ring, v_ring, PLANE)

    def around(*refs):
        windows(z, *refs)

    (columns,) = call(around, [((taps * c, cells), BF16)], 0, v_below, v_ring, v_above)
    piece = (pieces, taps * c // pieces, total // 2)
    keep, send, k_mine = call(
        weight_terms,
        [(piece, F32), (piece, F32), ((total, half_taps), BF16)],
        work,
        core,
        columns,
        received,
    )
    swap = [(0, 1), (1, 0)]
    (halves,) = call(add_halves, [(piece, F32)], 0, keep, lax.ppermute(send, "core", swap))

    halves, k_mine, received = lax.optimization_barrier((halves, k_mine, received))
    parts = exchange(halves, ("x", "sy"))
    k_other = lax.ppermute(k_mine, "core", swap)
    middle, ends = ((3 * c, cells), F32), ((3 * c, z), F32)

    def from_cotangent(*refs):
        spread_cotangent(z, *refs)

    def from_volume(*refs):
        spread_volume(z, *refs)

    g_middle, g_up, g_down = call(from_cotangent, [middle, ends, ends], work, received, k)
    (k_out,) = call(
        weights_by_output, [((taps * c, total), BF16)], 0, core, k_mine, k_other
    )
    both_ends = ((6 * c, z), F32)
    v_middle, up, down = call(
        from_volume, [middle, both_ends, both_ends], work, received, k_out, g_up, g_down
    )
    before, after = neighbours(up, down, "sy")
    parts, before, after = lax.optimization_barrier((parts, before, after))
    scale = math.sqrt(cells * devices)

    def reduce_pieces(*refs):
        sum_pieces(scale, *refs)

    (copies,) = call(reduce_pieces, [(piece, F32)], 0, parts)
    copies, before, after = lax.optimization_barrier((copies, before, after))
    mine = exchange(copies, ("x", "sy"))
    own, to_below, to_above = call(
        add_ends, [((2 * c, cells), F32)] * 3, 0, g_middle, v_middle, before, after
    )
    below, above = neighbours(to_above, to_below, PLANE)
    result = ((rows, c, z), BF16)
    out, grad_input = call(add_planes, [result, result], 0, own, below, above)
    mine, out, grad_input = lax.optimization_barrier((mine, out, grad_input))
    other = lax.ppermute(mine, "core", swap)
    (grad_kernel,) = call(join_halves, [((taps * c, total), F32)], 0, core, mine, other)
    return (
        out.transpose(0, 2, 1)[None],
        grad_input.transpose(0, 2, 1)[None],
        grad_kernel.reshape(taps, c, total),
    )


def solution(mesh):
    cores = 2
    shape = (mesh.shape["chan"], mesh.shape["sx"] // cores, cores, mesh.shape["sy"])
    split = Mesh(mesh.devices.reshape(shape), ("chan", "x", "core", "sy"))
    cells = P(PLANE, "sy", None, "chan")
    weights = P(None, "chan", None)
    return jax.shard_map(
        body,
        mesh=split,
        in_specs=(cells, weights, cells),
        out_specs=(cells, cells, weights),
        check_vma=False,
    )
```

```python
import math

import jax
import jax.numpy as jnp
from jax import lax
from jax.experimental import pallas as pl
from jax.experimental.pallas import tpu as pltpu
from jax.sharding import Mesh
from jax.sharding import PartitionSpec as P

F32 = jnp.float32
BF16 = jnp.bfloat16
PLANE = ("x", "core")
TAPS = 27
PARAMS = pltpu.CompilerParams(vmem_limit_bytes=16 * 2**20)


def call(kernel, outs, flops, *args):
    moved = sum(a.size * a.dtype.itemsize for a in args)
    moved += sum(math.prod(s) * jnp.dtype(d).itemsize for s, d in outs)
    specs = [
        pl.BlockSpec(memory_space=pltpu.SMEM if a.dtype == jnp.int32 else pltpu.VMEM) for a in args
    ]
    return pl.pallas_call(
        kernel,
        out_shape=[jax.ShapeDtypeStruct(s, d) for s, d in outs],
        in_specs=specs,
        out_specs=[pl.BlockSpec(memory_space=pltpu.VMEM) for _ in outs],
        compiler_params=PARAMS,
        cost_estimate=pl.CostEstimate(flops=flops, bytes_accessed=moved, transcendentals=0),
    )(*args)


def first_sends(core, v, g, k, first, last, sends, v_own, g_own, k_own, sems):
    rows, c, z = g_own.shape
    cells = rows * z
    skip = TAPS // 2 * c
    held = k.shape[0] - skip
    moves = [
        pltpu.make_async_copy(v, v_own, sems.at[0]),
        pltpu.make_async_copy(g, g_own, sems.at[1]),
        pltpu.make_async_copy(
            k.at[pl.ds(pl.multiple_of(core[0] * skip, c), held)], k_own.at[pl.ds(0, held)], sems.at[2]
        ),
    ]
    for move in moves:
        move.start()
    k_own[held:] = jnp.zeros((k_own.shape[0] - held, k_own.shape[1]), BF16)
    moves[0].wait()
    first[...] = v_own[0]
    last[...] = v_own[rows - 1]
    v_flat = in_row([v_own[r] for r in range(rows)])
    moves[1].wait()
    g_flat = in_row([g_own[r] for r in range(rows)])
    moves[2].wait()
    turned = k_own[...].astype(F32).T.astype(BF16)
    for at, to in enumerate(turn(sends.shape[0])):
        sends[at, :, :cells] = g_flat
        sends[at, :, cells : 2 * cells] = v_flat
        sends[at, :, 2 * cells :] = turned[to * c : (to + 1) * c]


def turn(groups):
    return [(at + 5) % groups for at in range(groups)]


def by_chan(received, start, size):
    order = turn(received.shape[0])
    blocks = [received[order.index(i)][:, start : start + size] for i in range(len(order))]
    return jnp.concatenate(blocks, axis=0)


def in_row(parts):
    return jnp.concatenate([part.astype(F32) for part in parts], axis=1).astype(BF16)


def volume_ring(v, before, after, ring):
    ring[...] = in_row([v[r] for r in range(v.shape[0])] + [after[...], before[...]])


def weights_by_output(core, mine, other, k_out):
    c = k_out.shape[0] // TAPS
    groups = mine.shape[0] // c
    middle = TAPS // 2
    is_low = core[0] == 0
    a, b = mine[...], other[...]
    for tap in range(TAPS):
        half = jnp.where(is_low, a, b) if tap < middle else jnp.where(is_low, b, a)
        at = (tap if tap < middle else tap - middle) * c
        blocks = [half[i * c : (i + 1) * c, at : at + c] for i in range(groups)]
        k_out[tap * c : (tap + 1) * c] = in_row(blocks)


def in_line(shape, z, shift):
    at = lax.broadcasted_iota(jnp.int32, shape, 1) % z + shift
    return (at >= 0) & (at < z)


def windows(z, below, own, above, columns):
    c = own.shape[0]
    lanes = own.shape[1]
    cells = lanes - 2 * z
    planes = jnp.concatenate([below[...], own[...], above[...]], axis=0).astype(F32)
    for e in range(3):
        moved = planes if e == 1 else pltpu.roll(planes, (1 - e) % lanes, 1)
        if e != 1:
            moved = jnp.where(in_line(moved.shape, z, e - 1), moved, 0.0)
        for b in range(3):
            window = moved if b == 1 else pltpu.roll(moved, (z * (1 - b)) % lanes, 1)
            window = window[:, :cells].astype(BF16)
            for a in range(3):
                at = (9 * a + 3 * b + e) * c
                columns[at : at + c, :] = window[a * c : (a + 1) * c]


def weight_terms(core, columns, received, keep, send, k_mine):
    groups, c, _ = received.shape
    cells, total = columns.shape[1], groups * c
    g_own = by_chan(received, 0, cells)
    terms = lax.dot_general(
        columns[...], g_own, (((1,), (1,)), ((), ())), preferred_element_type=F32
    )
    half = total // 2
    low, high = terms[:, :half], terms[:, half:]
    is_low = core[0] == 0
    kept = jnp.where(is_low, low, high)
    sent = jnp.where(is_low, high, low)
    pieces, rows = keep.shape[0], keep.shape[1]
    for piece in range(pieces):
        keep[piece] = kept[piece * rows : (piece + 1) * rows]
        send[piece] = sent[piece * rows : (piece + 1) * rows]
    k_mine[...] = by_chan(received, 2 * cells, k_mine.shape[1])


def spread(z, sign, own, k):
    lanes = own.shape[1] + 2 * z
    taps = k.shape[0] // 3
    c = taps // 9
    result = []
    for a in range(3)[:: -sign]:
        terms = jnp.dot(k[a * taps : (a + 1) * taps, :], own, preferred_element_type=F32)
        terms = jnp.concatenate([terms, jnp.zeros((taps, 2 * z), F32)], axis=1)
        plane = jnp.zeros((c, lanes), F32)
        for e in range(3):
            line = jnp.zeros((c, lanes), F32)
            for b in range(3):
                at = (3 * b + e) * c
                term = terms[at : at + c]
                line += term if b == 1 else pltpu.roll(term, (sign * z * (1 - b)) % lanes, 1)
            if e != 1:
                line = pltpu.roll(line, (sign * (1 - e)) % lanes, 1)
                line = jnp.where(in_line(line.shape, z, sign * (e - 1)), line, 0.0)
            plane += line
        result.append(plane)
    return result


def store_spread(planes, middle, up, down):
    c, cells = middle.shape[0] // 3, middle.shape[1]
    z = up.shape[1]
    for i, plane in enumerate(planes):
        at = slice(i * c, (i + 1) * c)
        middle[at] = plane[:, :cells]
        ends = plane[:, cells:]
        up[at] = ends[:, :z]
        down[at] = pltpu.roll(ends, z, 1)[:, :z]


def spread_cotangent(z, received, k, middle, up, down):
    cells = middle.shape[1]
    own = by_chan(received, 0, cells)
    store_spread(spread(z, -1, own, k), middle, up, down)


def spread_volume(z, received, k_out, g_up, g_down, middle, up, down):
    cells = middle.shape[1]
    own = by_chan(received, cells, cells)
    rows = g_up.shape[0]
    store_spread(spread(z, 1, own, k_out), middle, up.at[pl.ds(rows, rows)], down.at[pl.ds(rows, rows)])
    up[:rows] = g_up[...]
    down[:rows] = g_down[...]


def add_ends(g_middle, v_middle, before, after, own, to_below, to_above):
    rows, cells = g_middle.shape
    z, c = before.shape[1], rows // 3
    first = jnp.concatenate([before[...], jnp.zeros((2 * rows, z), F32)], axis=1)
    last = jnp.concatenate([jnp.zeros((2 * rows, z), F32), after[...]], axis=1)
    for i, middle in enumerate((g_middle, v_middle)):
        for part, out in enumerate((to_below, own, to_above)):
            at = slice(part * c, (part + 1) * c)
            from_end = slice(i * rows + part * c, i * rows + (part + 1) * c)
            value = middle[at]
            to = slice(i * c, (i + 1) * c)
            out[to] = value
            out[to, : 2 * z] = value[:, : 2 * z] + first[from_end]
            out[to, cells - 2 * z :] = value[:, cells - 2 * z :] + last[from_end]


def add_planes(own, below, above, out, grad_input):
    total = own[...] + below[...] + above[...]
    c = total.shape[0] // 2
    split_rows(total[c:], out)
    split_rows(total[:c], grad_input)


def split_rows(value, out):
    rows, z = out.shape[0], out.shape[2]
    lanes = value.shape[1]
    for r in range(rows):
        shifted = value if r == 0 else pltpu.roll(value, lanes - r * z, 1)
        out[r] = shifted[:, :z].astype(BF16)


def add_halves(keep, other, out):
    out[...] = keep[...] + other[...]


def sum_pieces(scale, parts, out):
    total = parts[0]
    for part in range(1, parts.shape[0]):
        total += parts[part]
    total = total / scale
    for copy in range(out.shape[0]):
        out[copy] = total


def join_halves(core, mine, other, out):
    pieces, rows, half = mine.shape
    first = core[0] == 0
    for piece in range(pieces):
        a, b = mine[piece], other[piece]
        out[piece * rows : (piece + 1) * rows, :half] = jnp.where(first, a, b)
        out[piece * rows : (piece + 1) * rows, half:] = jnp.where(first, b, a)


def neighbours(value_up, value_down, axis):
    n = lax.axis_size(axis)
    up = [(i, i + 1) for i in range(n - 1)]
    down = [(i + 1, i) for i in range(n - 1)]
    return lax.ppermute(value_up, axis, up), lax.ppermute(value_down, axis, down)


def exchange(value, axis):
    return lax.all_to_all(value, axis, 0, 0, tiled=True)


def body(volume, kernel, grad_out):
    _, rows, z, c = volume.shape
    taps, _, total = kernel.shape
    cells, lanes = rows * z, (rows + 2) * z
    groups = lax.axis_size("chan")
    pieces = lax.axis_size("x") * lax.axis_size("sy")
    devices = pieces * lax.axis_size("core")
    v = volume[0].transpose(0, 2, 1)
    g = grad_out[0].transpose(0, 2, 1)
    k = kernel.reshape(taps * c, total)
    core = lax.axis_index("core").reshape(1).astype(jnp.int32)
    work = 2 * taps * c * total * cells
    half_taps = (taps - taps // 2) * c
    weights = pl.cdiv(half_taps, 128) * 128
    width = 2 * cells + weights

    edge = jax.ShapeDtypeStruct((c, z), BF16)
    first, last, sends = pl.pallas_call(
        first_sends,
        out_shape=[edge, edge, jax.ShapeDtypeStruct((groups, c, width), BF16)],
        in_specs=[pl.BlockSpec(memory_space=pltpu.SMEM)]
        + [pl.BlockSpec(memory_space=pltpu.HBM)] * 3,
        out_specs=[pl.BlockSpec(memory_space=pltpu.VMEM)] * 3,
        scratch_shapes=[
            pltpu.VMEM((rows, c, z), BF16),
            pltpu.VMEM((rows, c, z), BF16),
            pltpu.VMEM((weights, total), BF16),
            pltpu.SemaphoreType.DMA((3,)),
        ],
        compiler_params=pltpu.CompilerParams(vmem_limit_bytes=60 * 2**20),
        cost_estimate=pl.CostEstimate(
            flops=0, bytes_accessed=groups * c * width * 4, transcendentals=0
        ),
    )(core, v, g, k)
    before, after = neighbours(last, first, "sy")
    received = lax.all_to_all(sends, "chan", 0, 0, axis_index_groups=[turn(groups)], tiled=True)
    (v_ring,) = call(volume_ring, [((c, lanes), BF16)], 0, v, before, after)
    v_below, v_above = neighbours(v_ring, v_ring, PLANE)

    def around(*refs):
        windows(z, *refs)

    (columns,) = call(around, [((taps * c, cells), BF16)], 0, v_below, v_ring, v_above)
    piece = (pieces, taps * c // pieces, total // 2)
    keep, send, k_mine = call(
        weight_terms,
        [(piece, F32), (piece, F32), ((total, half_taps), BF16)],
        work,
        core,
        columns,
        received,
    )
    swap = [(0, 1), (1, 0)]
    (halves,) = call(add_halves, [(piece, F32)], 0, keep, lax.ppermute(send, "core", swap))

    halves, k_mine, received = lax.optimization_barrier((halves, k_mine, received))
    parts = exchange(halves, ("x", "sy"))
    k_other = lax.ppermute(k_mine, "core", swap)
    middle, ends = ((3 * c, cells), F32), ((3 * c, z), F32)

    def from_cotangent(*refs):
        spread_cotangent(z, *refs)

    def from_volume(*refs):
        spread_volume(z, *refs)

    g_middle, g_up, g_down = call(from_cotangent, [middle, ends, ends], work, received, k)
    (k_out,) = call(
        weights_by_output, [((taps * c, total), BF16)], 0, core, k_mine, k_other
    )
    both_ends = ((6 * c, z), F32)
    v_middle, up, down = call(
        from_volume, [middle, both_ends, both_ends], work, received, k_out, g_up, g_down
    )
    before, after = neighbours(up, down, "sy")
    parts, before, after = lax.optimization_barrier((parts, before, after))
    scale = math.sqrt(cells * devices)

    def reduce_pieces(*refs):
        sum_pieces(scale, *refs)

    (copies,) = call(reduce_pieces, [(piece, F32)], 0, parts)
    copies, before, after = lax.optimization_barrier((copies, before, after))
    mine = exchange(copies, ("x", "sy"))
    own, to_below, to_above = call(
        add_ends, [((2 * c, cells), F32)] * 3, 0, g_middle, v_middle, before, after
    )
    below, above = neighbours(to_above, to_below, PLANE)
    result = ((rows, c, z), BF16)
    out, grad_input = call(add_planes, [result, result], 0, own, below, above)
    mine, out, grad_input = lax.optimization_barrier((mine, out, grad_input))
    other = lax.ppermute(mine, "core", swap)
    (grad_kernel,) = call(join_halves, [((taps * c, total), F32)], 0, core, mine, other)
    return (
        out.transpose(0, 2, 1)[None],
        grad_input.transpose(0, 2, 1)[None],
        grad_kernel.reshape(taps, c, total),
    )


def solution(mesh):
    cores = 2
    shape = (mesh.shape["chan"], mesh.shape["sx"] // cores, cores, mesh.shape["sy"])
    split = Mesh(mesh.devices.reshape(shape), ("chan", "x", "core", "sy"))
    cells = P(PLANE, "sy", None, "chan")
    weights = P(None, "chan", None)
    return jax.shard_map(
        body,
        mesh=split,
        in_specs=(cells, weights, cells),
        out_specs=(cells, cells, weights),
        check_vma=False,
    )
```

```python
import math

import jax
import jax.numpy as jnp
from jax import lax
from jax.experimental import pallas as pl
from jax.experimental.pallas import tpu as pltpu
from jax.sharding import Mesh
from jax.sharding import PartitionSpec as P

F32 = jnp.float32
BF16 = jnp.bfloat16
PLANE = ("x", "core")
TAPS = 27
PARAMS = pltpu.CompilerParams(vmem_limit_bytes=16 * 2**20)


def call(kernel, outs, flops, *args):
    moved = sum(a.size * a.dtype.itemsize for a in args)
    moved += sum(math.prod(s) * jnp.dtype(d).itemsize for s, d in outs)
    specs = [
        pl.BlockSpec(memory_space=pltpu.SMEM if a.dtype == jnp.int32 else pltpu.VMEM) for a in args
    ]
    return pl.pallas_call(
        kernel,
        out_shape=[jax.ShapeDtypeStruct(s, d) for s, d in outs],
        in_specs=specs,
        out_specs=[pl.BlockSpec(memory_space=pltpu.VMEM) for _ in outs],
        compiler_params=PARAMS,
        cost_estimate=pl.CostEstimate(flops=flops, bytes_accessed=moved, transcendentals=0),
    )(*args)


def first_sends(core, v, g, k, first, last, sends, v_own, g_own, k_own, sems):
    rows, c, z = g_own.shape
    cells = rows * z
    skip = TAPS // 2 * c
    held = k.shape[0] - skip
    moves = [
        pltpu.make_async_copy(v, v_own, sems.at[0]),
        pltpu.make_async_copy(g, g_own, sems.at[1]),
        pltpu.make_async_copy(
            k.at[pl.ds(pl.multiple_of(core[0] * skip, c), held)], k_own.at[pl.ds(0, held)], sems.at[2]
        ),
    ]
    for move in moves:
        move.start()
    k_own[held:] = jnp.zeros((k_own.shape[0] - held, k_own.shape[1]), BF16)
    moves[0].wait()
    first[...] = v_own[0]
    last[...] = v_own[rows - 1]
    v_flat = in_row([v_own[r] for r in range(rows)])
    moves[1].wait()
    g_flat = in_row([g_own[r] for r in range(rows)])
    moves[2].wait()
    turned = k_own[...].astype(F32).T.astype(BF16)
    for at, to in enumerate(turn(sends.shape[0])):
        sends[at, :, :cells] = g_flat
        sends[at, :, cells : 2 * cells] = v_flat
        sends[at, :, 2 * cells :] = turned[to * c : (to + 1) * c]


def turn(groups):
    return [(at + 5) % groups for at in range(groups)]


def by_chan(received, start, size):
    order = turn(received.shape[0])
    blocks = [received[order.index(i)][:, start : start + size] for i in range(len(order))]
    return jnp.concatenate(blocks, axis=0)


def in_row(parts):
    return jnp.concatenate([part.astype(F32) for part in parts], axis=1).astype(BF16)


def volume_ring(v, before, after, ring):
    ring[...] = in_row([v[r] for r in range(v.shape[0])] + [after[...], before[...]])


def weights_by_output(core, mine, other, k_out):
    c = k_out.shape[0] // TAPS
    groups = mine.shape[0] // c
    middle = TAPS // 2
    is_low = core[0] == 0
    a, b = mine[...], other[...]
    for tap in range(TAPS):
        half = jnp.where(is_low, a, b) if tap < middle else jnp.where(is_low, b, a)
        at = (tap if tap < middle else tap - middle) * c
        blocks = [half[i * c : (i + 1) * c, at : at + c] for i in range(groups)]
        k_out[tap * c : (tap + 1) * c] = in_row(blocks)


def in_line(shape, z, shift):
    at = lax.broadcasted_iota(jnp.int32, shape, 1) % z + shift
    return (at >= 0) & (at < z)


def windows(z, below, own, above, columns):
    c = own.shape[0]
    lanes = own.shape[1]
    cells = lanes - 2 * z
    planes = jnp.concatenate([below[...], own[...], above[...]], axis=0).astype(F32)
    for e in range(3):
        moved = planes if e == 1 else pltpu.roll(planes, (1 - e) % lanes, 1)
        if e != 1:
            moved = jnp.where(in_line(moved.shape, z, e - 1), moved, 0.0)
        for b in range(3):
            window = moved if b == 1 else pltpu.roll(moved, (z * (1 - b)) % lanes, 1)
            window = window[:, :cells].astype(BF16)
            for a in range(3):
                at = (9 * a + 3 * b + e) * c
                columns[at : at + c, :] = window[a * c : (a + 1) * c]


def weight_terms(core, columns, received, keep, send, k_mine):
    groups, c, _ = received.shape
    cells, total = columns.shape[1], groups * c
    g_own = by_chan(received, 0, cells)
    terms = lax.dot_general(
        columns[...], g_own, (((1,), (1,)), ((), ())), preferred_element_type=F32
    )
    half = total // 2
    low, high = terms[:, :half], terms[:, half:]
    is_low = core[0] == 0
    keep[...] = jnp.where(is_low, low, high)
    send[...] = jnp.where(is_low, high, low)
    k_mine[...] = by_chan(received, 2 * cells, k_mine.shape[1])


def spread(z, sign, own, k):
    lanes = own.shape[1] + 2 * z
    taps = k.shape[0] // 3
    c = taps // 9
    result = []
    for a in range(3)[:: -sign]:
        terms = jnp.dot(k[a * taps : (a + 1) * taps, :], own, preferred_element_type=F32)
        terms = jnp.concatenate([terms, jnp.zeros((taps, 2 * z), F32)], axis=1)
        plane = jnp.zeros((c, lanes), F32)
        for e in range(3):
            line = jnp.zeros((c, lanes), F32)
            for b in range(3):
                at = (3 * b + e) * c
                term = terms[at : at + c]
                line += term if b == 1 else pltpu.roll(term, (sign * z * (1 - b)) % lanes, 1)
            if e != 1:
                line = pltpu.roll(line, (sign * (1 - e)) % lanes, 1)
                line = jnp.where(in_line(line.shape, z, sign * (e - 1)), line, 0.0)
            plane += line
        result.append(plane)
    return result


def store_spread(planes, middle):
    c, cells = middle.shape[0] // 3, middle.shape[1]
    for i, plane in enumerate(planes):
        middle[i * c : (i + 1) * c] = plane[:, :cells]
    ends = jnp.concatenate([plane[:, cells:] for plane in planes], axis=0)
    z = ends.shape[1] // 2
    return ends, pltpu.roll(ends, z, 1)


def is_low_half(shape):
    return lax.broadcasted_iota(jnp.int32, shape, 1) < shape[1] // 2


def spread_cotangent(z, received, k, middle, ends):
    own = by_chan(received, 0, middle.shape[1])
    ends[...], _ = store_spread(spread(z, -1, own, k), middle)


def spread_volume(z, received, k_out, g_ends, middle, up, down):
    cells = middle.shape[1]
    own = by_chan(received, cells, cells)
    ends, turned = store_spread(spread(z, 1, own, k_out), middle)
    low = is_low_half(ends.shape)
    up[...] = jnp.where(low, g_ends[...], turned)
    down[...] = jnp.where(low, pltpu.roll(g_ends[...], z, 1), ends)


def add_ends(g_middle, v_middle, before, after, own, to_below, to_above):
    rows, cells = g_middle.shape
    width = before.shape[1]
    c = rows // 3
    low = is_low_half(before.shape)
    g_first, v_last = before[...], after[...]
    v_first, g_last = pltpu.roll(g_first, width // 2, 1), pltpu.roll(v_last, width // 2, 1)
    for i, (middle, first, last) in enumerate(
        ((g_middle, g_first, g_last), (v_middle, v_first, v_last))
    ):
        first = jnp.where(low, first, 0.0)
        last = jnp.where(low, 0.0, last)
        for part, out in enumerate((to_below, own, to_above)):
            at = slice(part * c, (part + 1) * c)
            to = slice(i * c, (i + 1) * c)
            out[to] = middle[at]
            out[to, :width] = middle[at, :width] + first[at]
            out[to, cells - width :] = middle[at, cells - width :] + last[at]


def add_planes(own, below, above, out, grad_input):
    total = own[...] + below[...] + above[...]
    c = total.shape[0] // 2
    split_rows(total[c:], out)
    split_rows(total[:c], grad_input)


def split_rows(value, out):
    rows, z = out.shape[0], out.shape[2]
    lanes = value.shape[1]
    for r in range(rows):
        shifted = value if r == 0 else pltpu.roll(value, lanes - r * z, 1)
        out[r] = shifted[:, :z].astype(BF16)


def add_halves(keep, other, out):
    out[...] = keep[...] + other[...]


def sum_pieces(scale, pieces, parts, out):
    rows = parts.shape[0] // pieces
    total = parts[:rows]
    for at in range(rows, rows * pieces, rows):
        total += parts[at : at + rows]
    total = total / scale
    for at in range(0, rows * pieces, rows):
        out[at : at + rows] = total


def join_halves(core, mine, other, out):
    half = mine.shape[1]
    is_low = core[0] == 0
    out[:, :half] = jnp.where(is_low, mine[...], other[...])
    out[:, half:] = jnp.where(is_low, other[...], mine[...])


def neighbours(value_up, value_down, axis):
    n = lax.axis_size(axis)
    up = [(i, i + 1) for i in range(n - 1)]
    down = [(i + 1, i) for i in range(n - 1)]
    return lax.ppermute(value_up, axis, up), lax.ppermute(value_down, axis, down)


def exchange_rows(value, axis):
    apart = value.reshape(value.shape[0], 1, value.shape[1])
    return lax.all_to_all(apart, axis, 0, 0, tiled=True).reshape(value.shape)


def body(volume, kernel, grad_out):
    _, rows, z, c = volume.shape
    taps, _, total = kernel.shape
    cells, lanes = rows * z, (rows + 2) * z
    groups = lax.axis_size("chan")
    pieces = lax.axis_size("x") * lax.axis_size("sy")
    devices = pieces * lax.axis_size("core")
    v = volume[0].transpose(0, 2, 1)
    g = grad_out[0].transpose(0, 2, 1)
    k = kernel.reshape(taps * c, total)
    core = lax.axis_index("core").reshape(1).astype(jnp.int32)
    work = 2 * taps * c * total * cells
    half_taps = (taps - taps // 2) * c
    weights = pl.cdiv(half_taps, 128) * 128
    width = 2 * cells + weights

    edge = jax.ShapeDtypeStruct((c, z), BF16)
    first, last, sends = pl.pallas_call(
        first_sends,
        out_shape=[edge, edge, jax.ShapeDtypeStruct((groups, c, width), BF16)],
        in_specs=[pl.BlockSpec(memory_space=pltpu.SMEM)]
        + [pl.BlockSpec(memory_space=pltpu.HBM)] * 3,
        out_specs=[pl.BlockSpec(memory_space=pltpu.VMEM)] * 3,
        scratch_shapes=[
            pltpu.VMEM((rows, c, z), BF16),
            pltpu.VMEM((rows, c, z), BF16),
            pltpu.VMEM((weights, total), BF16),
            pltpu.SemaphoreType.DMA((3,)),
        ],
        compiler_params=pltpu.CompilerParams(vmem_limit_bytes=60 * 2**20),
        cost_estimate=pl.CostEstimate(
            flops=0, bytes_accessed=groups * c * width * 4, transcendentals=0
        ),
    )(core, v, g, k)
    before, after = neighbours(last, first, "sy")
    received = lax.all_to_all(sends, "chan", 0, 0, axis_index_groups=[turn(groups)], tiled=True)
    (v_ring,) = call(volume_ring, [((c, lanes), BF16)], 0, v, before, after)
    v_below, v_above = neighbours(v_ring, v_ring, PLANE)

    def around(*refs):
        windows(z, *refs)

    (columns,) = call(around, [((taps * c, cells), BF16)], 0, v_below, v_ring, v_above)
    piece = (taps * c, total // 2)
    keep, send, k_mine = call(
        weight_terms,
        [(piece, F32), (piece, F32), ((total, half_taps), BF16)],
        work,
        core,
        columns,
        received,
    )
    swap = [(0, 1), (1, 0)]
    (halves,) = call(add_halves, [(piece, F32)], 0, keep, lax.ppermute(send, "core", swap))

    halves, k_mine, received = lax.optimization_barrier((halves, k_mine, received))
    parts = exchange_rows(halves, ("x", "sy"))
    k_other = lax.ppermute(k_mine, "core", swap)
    middle, ends = ((3 * c, cells), F32), ((3 * c, 2 * z), F32)

    def from_cotangent(*refs):
        spread_cotangent(z, *refs)

    def from_volume(*refs):
        spread_volume(z, *refs)

    g_middle, g_ends = call(from_cotangent, [middle, ends], work, received, k)
    (k_out,) = call(weights_by_output, [((taps * c, total), BF16)], 0, core, k_mine, k_other)
    v_middle, up, down = call(
        from_volume, [middle, ends, ends], work, received, k_out, g_ends
    )
    before, after = neighbours(up, down, "sy")
    parts, before, after = lax.optimization_barrier((parts, before, after))
    scale = math.sqrt(cells * devices)

    def reduce_pieces(*refs):
        sum_pieces(scale, pieces, *refs)

    (copies,) = call(reduce_pieces, [(piece, F32)], 0, parts)
    copies, before, after = lax.optimization_barrier((copies, before, after))
    mine = exchange_rows(copies, ("x", "sy"))
    own, to_below, to_above = call(
        add_ends, [((2 * c, cells), F32)] * 3, 0, g_middle, v_middle, before, after
    )
    below, above = neighbours(to_above, to_below, PLANE)
    result = ((rows, c, z), BF16)
    mine, below, above = lax.optimization_barrier((mine, below, above))
    out, grad_input = call(add_planes, [result, result], 0, own, below, above)
    other = lax.ppermute(mine, "core", swap)
    (grad_kernel,) = call(join_halves, [((taps * c, total), F32)], 0, core, mine, other)
    return (
        out.transpose(0, 2, 1)[None],
        grad_input.transpose(0, 2, 1)[None],
        grad_kernel.reshape(taps, c, total),
    )


def solution(mesh):
    cores = 2
    shape = (mesh.shape["chan"], mesh.shape["sx"] // cores, cores, mesh.shape["sy"])
    split = Mesh(mesh.devices.reshape(shape), ("chan", "x", "core", "sy"))
    cells = P(PLANE, "sy", None, "chan")
    weights = P(None, "chan", None)
    return jax.shard_map(
        body,
        mesh=split,
        in_specs=(cells, weights, cells),
        out_specs=(cells, cells, weights),
        check_vma=False,
    )
```

```python
import math

import jax
import jax.numpy as jnp
from jax import lax
from jax.experimental import pallas as pl
from jax.experimental.pallas import tpu as pltpu
from jax.sharding import Mesh
from jax.sharding import PartitionSpec as P

F32 = jnp.float32
BF16 = jnp.bfloat16
PLANE = ("x", "core")
TAPS = 27
PARAMS = pltpu.CompilerParams(vmem_limit_bytes=16 * 2**20)


def call(kernel, outs, flops, *args):
    moved = sum(a.size * a.dtype.itemsize for a in args)
    moved += sum(math.prod(s) * jnp.dtype(d).itemsize for s, d in outs)
    specs = [
        pl.BlockSpec(memory_space=pltpu.SMEM if a.dtype == jnp.int32 else pltpu.VMEM) for a in args
    ]
    return pl.pallas_call(
        kernel,
        out_shape=[jax.ShapeDtypeStruct(s, d) for s, d in outs],
        in_specs=specs,
        out_specs=[pl.BlockSpec(memory_space=pltpu.VMEM) for _ in outs],
        compiler_params=PARAMS,
        cost_estimate=pl.CostEstimate(flops=flops, bytes_accessed=moved, transcendentals=0),
    )(*args)


def first_sends(core, v, g, k, first, last, sends, v_own, g_own, k_own, sems):
    rows, c, z = g_own.shape
    cells = rows * z
    skip = TAPS // 2 * c
    held = k.shape[0] - skip
    moves = [
        pltpu.make_async_copy(v, v_own, sems.at[0]),
        pltpu.make_async_copy(g, g_own, sems.at[1]),
        pltpu.make_async_copy(
            k.at[pl.ds(pl.multiple_of(core[0] * skip, c), held)], k_own.at[pl.ds(0, held)], sems.at[2]
        ),
    ]
    for move in moves:
        move.start()
    k_own[held:] = jnp.zeros((k_own.shape[0] - held, k_own.shape[1]), BF16)
    moves[0].wait()
    first[...] = v_own[0]
    last[...] = v_own[rows - 1]
    v_flat = in_row([v_own[r] for r in range(rows)])
    moves[1].wait()
    g_flat = in_row([g_own[r] for r in range(rows)])
    moves[2].wait()
    turned = k_own[...].T
    for at, to in enumerate(turn(sends.shape[0])):
        sends[at, :, :cells] = g_flat
        sends[at, :, cells : 2 * cells] = v_flat
        sends[at, :, 2 * cells :] = turned[to * c : (to + 1) * c]


def turn(groups):
    return [(at + 5) % groups for at in range(groups)]


def by_chan(received, start, size):
    order = turn(received.shape[0])
    blocks = [received[order.index(i)][:, start : start + size] for i in range(len(order))]
    return jnp.concatenate(blocks, axis=0)


def in_row(parts):
    return jnp.concatenate(parts, axis=1)


def volume_ring(v, before, after, ring):
    ring[...] = in_row([v[r] for r in range(v.shape[0])] + [after[...], before[...]])


def weights_by_output(core, mine, other, k_out):
    c = k_out.shape[0] // TAPS
    groups = mine.shape[0] // c
    middle = TAPS // 2
    is_low = core[0] == 0
    a, b = mine[...], other[...]
    for tap in range(TAPS):
        half = jnp.where(is_low, a, b) if tap < middle else jnp.where(is_low, b, a)
        at = (tap if tap < middle else tap - middle) * c
        blocks = [half[i * c : (i + 1) * c, at : at + c] for i in range(groups)]
        k_out[tap * c : (tap + 1) * c] = in_row(blocks)


def in_line(shape, z, shift):
    at = lax.broadcasted_iota(jnp.int32, shape, 1) % z + shift
    return (at >= 0) & (at < z)


def windows(z, below, own, above, columns):
    c = own.shape[0]
    lanes = own.shape[1]
    cells = lanes - 2 * z
    planes = jnp.concatenate([below[...], own[...], above[...]], axis=0).astype(F32)
    for e in range(3):
        moved = planes if e == 1 else pltpu.roll(planes, (1 - e) % lanes, 1)
        if e != 1:
            moved = jnp.where(in_line(moved.shape, z, e - 1), moved, 0.0)
        for b in range(3):
            window = moved if b == 1 else pltpu.roll(moved, (z * (1 - b)) % lanes, 1)
            window = window[:, :cells].astype(BF16)
            for a in range(3):
                at = (9 * a + 3 * b + e) * c
                columns[at : at + c, :] = window[a * c : (a + 1) * c]


def weight_terms(core, columns, received, keep, send, k_mine):
    groups, c, _ = received.shape
    cells, total = columns.shape[1], groups * c
    g_own = by_chan(received, 0, cells)
    terms = lax.dot_general(
        columns[...], g_own, (((1,), (1,)), ((), ())), preferred_element_type=F32
    )
    half = total // 2
    low, high = terms[:, :half], terms[:, half:]
    is_low = core[0] == 0
    keep[...] = jnp.where(is_low, low, high)
    send[...] = jnp.where(is_low, high, low)
    k_mine[...] = by_chan(received, 2 * cells, k_mine.shape[1])


def spread(z, sign, own, k):
    lanes = own.shape[1] + 2 * z
    taps = k.shape[0] // 3
    c = taps // 9
    result = []
    for a in range(3)[:: -sign]:
        terms = jnp.dot(k[a * taps : (a + 1) * taps, :], own, preferred_element_type=F32)
        terms = jnp.concatenate([terms, jnp.zeros((taps, 2 * z), F32)], axis=1)
        plane = jnp.zeros((c, lanes), F32)
        for e in range(3):
            line = jnp.zeros((c, lanes), F32)
            for b in range(3):
                at = (3 * b + e) * c
                term = terms[at : at + c]
                line += term if b == 1 else pltpu.roll(term, (sign * z * (1 - b)) % lanes, 1)
            if e != 1:
                line = pltpu.roll(line, (sign * (1 - e)) % lanes, 1)
                line = jnp.where(in_line(line.shape, z, sign * (e - 1)), line, 0.0)
            plane += line
        result.append(plane)
    return result


def store_spread(planes, middle):
    c, cells = middle.shape[0] // 3, middle.shape[1]
    for i, plane in enumerate(planes):
        middle[i * c : (i + 1) * c] = plane[:, :cells]
    ends = jnp.concatenate([plane[:, cells:] for plane in planes], axis=0)
    z = ends.shape[1] // 2
    return ends, pltpu.roll(ends, z, 1)


def is_low_half(shape):
    return lax.broadcasted_iota(jnp.int32, shape, 1) < shape[1] // 2


def spread_cotangent(z, received, k, middle, ends):
    own = by_chan(received, 0, middle.shape[1])
    ends[...], _ = store_spread(spread(z, -1, own, k), middle)


def spread_volume(z, received, k_out, g_ends, middle, up, down):
    cells = middle.shape[1]
    own = by_chan(received, cells, cells)
    ends, turned = store_spread(spread(z, 1, own, k_out), middle)
    low = is_low_half(ends.shape)
    up[...] = jnp.where(low, g_ends[...], turned)
    down[...] = jnp.where(low, pltpu.roll(g_ends[...], z, 1), ends)


def add_ends(g_middle, v_middle, before, after, own, to_below, to_above):
    rows, cells = g_middle.shape
    width = before.shape[1]
    c = rows // 3
    low = is_low_half(before.shape)
    g_first, v_last = before[...], after[...]
    v_first, g_last = pltpu.roll(g_first, width // 2, 1), pltpu.roll(v_last, width // 2, 1)
    for i, (middle, first, last) in enumerate(
        ((g_middle, g_first, g_last), (v_middle, v_first, v_last))
    ):
        first = jnp.where(low, first, 0.0)
        last = jnp.where(low, 0.0, last)
        for part, out in enumerate((to_below, own, to_above)):
            at = slice(part * c, (part + 1) * c)
            to = slice(i * c, (i + 1) * c)
            out[to] = middle[at]
            out[to, :width] = middle[at, :width] + first[at]
            out[to, cells - width :] = middle[at, cells - width :] + last[at]


def add_planes(own, below, above, out, grad_input):
    total = own[...] + below[...] + above[...]
    c = total.shape[0] // 2
    split_rows(total[c:], out)
    split_rows(total[:c], grad_input)


def split_rows(value, out):
    rows, z = out.shape[0], out.shape[2]
    lanes = value.shape[1]
    for r in range(rows):
        shifted = value if r == 0 else pltpu.roll(value, lanes - r * z, 1)
        out[r] = shifted[:, :z].astype(BF16)


def add_halves(keep, other, out):
    out[...] = keep[...] + other[...]


def sum_pieces(scale, pieces, parts, out):
    rows = parts.shape[0] // pieces
    total = parts[:rows]
    for at in range(rows, rows * pieces, rows):
        total += parts[at : at + rows]
    total = total / scale
    for at in range(0, rows * pieces, rows):
        out[at : at + rows] = total


def join_halves(core, mine, other, out):
    half = mine.shape[1]
    is_low = core[0] == 0
    out[:, :half] = jnp.where(is_low, mine[...], other[...])
    out[:, half:] = jnp.where(is_low, other[...], mine[...])


def neighbours(value_up, value_down, axis):
    n = lax.axis_size(axis)
    up = [(i, i + 1) for i in range(n - 1)]
    down = [(i + 1, i) for i in range(n - 1)]
    return lax.ppermute(value_up, axis, up), lax.ppermute(value_down, axis, down)


def exchange_rows(value, axis):
    apart = value.reshape(value.shape[0], 1, value.shape[1])
    return lax.all_to_all(apart, axis, 0, 0, tiled=True).reshape(value.shape)


def body(volume, kernel, grad_out):
    _, rows, z, c = volume.shape
    taps, _, total = kernel.shape
    cells, lanes = rows * z, (rows + 2) * z
    groups = lax.axis_size("chan")
    pieces = lax.axis_size("x") * lax.axis_size("sy")
    devices = pieces * lax.axis_size("core")
    v = volume[0].transpose(0, 2, 1)
    g = grad_out[0].transpose(0, 2, 1)
    k = kernel.reshape(taps * c, total)
    core = lax.axis_index("core").reshape(1).astype(jnp.int32)
    work = 2 * taps * c * total * cells
    half_taps = (taps - taps // 2) * c
    weights = pl.cdiv(half_taps, 128) * 128
    width = 2 * cells + weights

    edge = jax.ShapeDtypeStruct((c, z), BF16)
    first, last, sends = pl.pallas_call(
        first_sends,
        out_shape=[edge, edge, jax.ShapeDtypeStruct((groups, c, width), BF16)],
        in_specs=[pl.BlockSpec(memory_space=pltpu.SMEM)]
        + [pl.BlockSpec(memory_space=pltpu.HBM)] * 3,
        out_specs=[pl.BlockSpec(memory_space=pltpu.VMEM)] * 3,
        scratch_shapes=[
            pltpu.VMEM((rows, c, z), BF16),
            pltpu.VMEM((rows, c, z), BF16),
            pltpu.VMEM((weights, total), BF16),
            pltpu.SemaphoreType.DMA((3,)),
        ],
        compiler_params=pltpu.CompilerParams(vmem_limit_bytes=60 * 2**20),
        cost_estimate=pl.CostEstimate(
            flops=0, bytes_accessed=groups * c * width * 4, transcendentals=0
        ),
    )(core, v, g, k)
    before, after = neighbours(last, first, "sy")
    received = lax.all_to_all(sends, "chan", 0, 0, axis_index_groups=[turn(groups)], tiled=True)
    (v_ring,) = call(volume_ring, [((c, lanes), BF16)], 0, v, before, after)
    v_below, v_above = neighbours(v_ring, v_ring, PLANE)

    def around(*refs):
        windows(z, *refs)

    (columns,) = call(around, [((taps * c, cells), BF16)], 0, v_below, v_ring, v_above)
    piece = (taps * c, total // 2)
    keep, send, k_mine = call(
        weight_terms,
        [(piece, F32), (piece, F32), ((total, half_taps), BF16)],
        work,
        core,
        columns,
        received,
    )
    swap = [(0, 1), (1, 0)]
    (halves,) = call(add_halves, [(piece, F32)], 0, keep, lax.ppermute(send, "core", swap))

    halves, k_mine, received = lax.optimization_barrier((halves, k_mine, received))
    parts = exchange_rows(halves, ("x", "sy"))
    k_other = lax.ppermute(k_mine, "core", swap)
    middle, ends = ((3 * c, cells), F32), ((3 * c, 2 * z), F32)

    def from_cotangent(*refs):
        spread_cotangent(z, *refs)

    def from_volume(*refs):
        spread_volume(z, *refs)

    g_middle, g_ends = call(from_cotangent, [middle, ends], work, received, k)
    (k_out,) = call(weights_by_output, [((taps * c, total), BF16)], 0, core, k_mine, k_other)
    v_middle, up, down = call(
        from_volume, [middle, ends, ends], work, received, k_out, g_ends
    )
    before, after = neighbours(up, down, "sy")
    parts, before, after = lax.optimization_barrier((parts, before, after))
    scale = math.sqrt(cells * devices)

    def reduce_pieces(*refs):
        sum_pieces(scale, pieces, *refs)

    (copies,) = call(reduce_pieces, [(piece, F32)], 0, parts)
    copies, before, after = lax.optimization_barrier((copies, before, after))
    mine = exchange_rows(copies, ("x", "sy"))
    own, to_below, to_above = call(
        add_ends, [((2 * c, cells), F32)] * 3, 0, g_middle, v_middle, before, after
    )
    below, above = neighbours(to_above, to_below, PLANE)
    result = ((rows, c, z), BF16)
    mine, below, above = lax.optimization_barrier((mine, below, above))
    out, grad_input = call(add_planes, [result, result], 0, own, below, above)
    other = lax.ppermute(mine, "core", swap)
    (grad_kernel,) = call(join_halves, [((taps * c, total), F32)], 0, core, mine, other)
    return (
        out.transpose(0, 2, 1)[None],
        grad_input.transpose(0, 2, 1)[None],
        grad_kernel.reshape(taps, c, total),
    )


def solution(mesh):
    cores = 2
    shape = (mesh.shape["chan"], mesh.shape["sx"] // cores, cores, mesh.shape["sy"])
    split = Mesh(mesh.devices.reshape(shape), ("chan", "x", "core", "sy"))
    cells = P(PLANE, "sy", None, "chan")
    weights = P(None, "chan", None)
    return jax.shard_map(
        body,
        mesh=split,
        in_specs=(cells, weights, cells),
        out_specs=(cells, cells, weights),
        check_vma=False,
    )
```

```python
import math

import jax
import jax.numpy as jnp
from jax import lax
from jax.experimental import pallas as pl
from jax.experimental.pallas import tpu as pltpu
from jax.sharding import Mesh
from jax.sharding import PartitionSpec as P

F32 = jnp.float32
BF16 = jnp.bfloat16
PLANE = ("x", "core")
TAPS = 27
PARAMS = pltpu.CompilerParams(vmem_limit_bytes=16 * 2**20)


def call(kernel, outs, flops, *args):
    moved = sum(a.size * a.dtype.itemsize for a in args)
    moved += sum(math.prod(s) * jnp.dtype(d).itemsize for s, d in outs)
    specs = [
        pl.BlockSpec(memory_space=pltpu.SMEM if a.dtype == jnp.int32 else pltpu.VMEM) for a in args
    ]
    return pl.pallas_call(
        kernel,
        out_shape=[jax.ShapeDtypeStruct(s, d) for s, d in outs],
        in_specs=specs,
        out_specs=[pl.BlockSpec(memory_space=pltpu.VMEM) for _ in outs],
        compiler_params=PARAMS,
        cost_estimate=pl.CostEstimate(flops=flops, bytes_accessed=moved, transcendentals=0),
    )(*args)


def first_sends(core, v, g, k, first, last, sends, v_own, g_own, k_own, sems):
    rows, c, z = g_own.shape
    cells = rows * z
    skip = TAPS // 2 * c
    held = k.shape[0] - skip
    moves = [
        pltpu.make_async_copy(v, v_own, sems.at[0]),
        pltpu.make_async_copy(g, g_own, sems.at[1]),
        pltpu.make_async_copy(
            k.at[pl.ds(pl.multiple_of(core[0] * skip, c), held)], k_own.at[pl.ds(0, held)], sems.at[2]
        ),
    ]
    for move in moves[::-1]:
        move.start()
    k_own[held:] = jnp.zeros((k_own.shape[0] - held, k_own.shape[1]), BF16)
    moves[0].wait()
    first[...] = v_own[0]
    last[...] = v_own[rows - 1]
    v_flat = in_row([v_own[r] for r in range(rows)])
    moves[1].wait()
    g_flat = in_row([g_own[r] for r in range(rows)])
    moves[2].wait()
    turned = k_own[...].T
    for at, to in enumerate(turn(sends.shape[0])):
        sends[at, :, :cells] = g_flat
        sends[at, :, cells : 2 * cells] = v_flat
        sends[at, :, 2 * cells :] = turned[to * c : (to + 1) * c]


def turn(groups):
    return [(at + 5) % groups for at in range(groups)]


def by_chan(received, start, size):
    order = turn(received.shape[0])
    blocks = [received[order.index(i)][:, start : start + size] for i in range(len(order))]
    return jnp.concatenate(blocks, axis=0)


def in_row(parts):
    return jnp.concatenate(parts, axis=1)


def volume_ring(v, before, after, ring):
    ring[...] = in_row([v[r] for r in range(v.shape[0])] + [after[...], before[...]])


def weights_by_output(core, mine, other, k_out):
    c = k_out.shape[0] // TAPS
    groups = mine.shape[0] // c
    middle = TAPS // 2
    is_low = core[0] == 0
    a, b = mine[...], other[...]
    for tap in range(TAPS):
        half = jnp.where(is_low, a, b) if tap < middle else jnp.where(is_low, b, a)
        at = (tap if tap < middle else tap - middle) * c
        blocks = [half[i * c : (i + 1) * c, at : at + c] for i in range(groups)]
        k_out[tap * c : (tap + 1) * c] = in_row(blocks)


def in_line(shape, z, shift):
    at = lax.broadcasted_iota(jnp.int32, shape, 1) % z + shift
    return (at >= 0) & (at < z)


def windows(z, below, own, above, columns):
    c = own.shape[0]
    lanes = own.shape[1]
    cells = lanes - 2 * z
    planes = jnp.concatenate([below[...], own[...], above[...]], axis=0).astype(F32)
    for e in range(3):
        moved = planes if e == 1 else pltpu.roll(planes, (1 - e) % lanes, 1)
        if e != 1:
            moved = jnp.where(in_line(moved.shape, z, e - 1), moved, 0.0)
        for b in range(3):
            window = moved if b == 1 else pltpu.roll(moved, (z * (1 - b)) % lanes, 1)
            window = window[:, :cells].astype(BF16)
            for a in range(3):
                at = (9 * a + 3 * b + e) * c
                columns[at : at + c, :] = window[a * c : (a + 1) * c]


def weight_terms(core, columns, received, keep, send, k_mine):
    groups, c, _ = received.shape
    cells, total = columns.shape[1], groups * c
    g_own = by_chan(received, 0, cells)
    terms = lax.dot_general(
        columns[...], g_own, (((1,), (1,)), ((), ())), preferred_element_type=F32
    )
    half = total // 2
    low, high = terms[:, :half], terms[:, half:]
    is_low = core[0] == 0
    keep[...] = jnp.where(is_low, low, high)
    send[...] = jnp.where(is_low, high, low)
    k_mine[...] = by_chan(received, 2 * cells, k_mine.shape[1])


def spread(z, sign, own, k):
    lanes = own.shape[1] + 2 * z
    taps = k.shape[0] // 3
    c = taps // 9
    result = []
    for a in range(3)[:: -sign]:
        terms = jnp.dot(k[a * taps : (a + 1) * taps, :], own, preferred_element_type=F32)
        terms = jnp.concatenate([terms, jnp.zeros((taps, 2 * z), F32)], axis=1)
        plane = jnp.zeros((c, lanes), F32)
        for e in range(3):
            line = jnp.zeros((c, lanes), F32)
            for b in range(3):
                at = (3 * b + e) * c
                term = terms[at : at + c]
                line += term if b == 1 else pltpu.roll(term, (sign * z * (1 - b)) % lanes, 1)
            if e != 1:
                line = pltpu.roll(line, (sign * (1 - e)) % lanes, 1)
                line = jnp.where(in_line(line.shape, z, sign * (e - 1)), line, 0.0)
            plane += line
        result.append(plane)
    return result


def store_spread(planes, middle):
    c, cells = middle.shape[0] // 3, middle.shape[1]
    for i, plane in enumerate(planes):
        middle[i * c : (i + 1) * c] = plane[:, :cells]
    ends = jnp.concatenate([plane[:, cells:] for plane in planes], axis=0)
    z = ends.shape[1] // 2
    return ends, pltpu.roll(ends, z, 1)


def is_low_half(shape):
    return lax.broadcasted_iota(jnp.int32, shape, 1) < shape[1] // 2


def spread_cotangent(z, received, k, middle, ends):
    own = by_chan(received, 0, middle.shape[1])
    ends[...], _ = store_spread(spread(z, -1, own, k), middle)


def spread_volume(z, received, k_out, g_ends, middle, up, down):
    cells = middle.shape[1]
    own = by_chan(received, cells, cells)
    ends, turned = store_spread(spread(z, 1, own, k_out), middle)
    low = is_low_half(ends.shape)
    up[...] = jnp.where(low, g_ends[...], turned)
    down[...] = jnp.where(low, pltpu.roll(g_ends[...], z, 1), ends)


def add_ends(g_middle, v_middle, before, after, own, to_below, to_above):
    rows, cells = g_middle.shape
    width = before.shape[1]
    c = rows // 3
    low = is_low_half(before.shape)
    g_first, v_last = before[...], after[...]
    v_first, g_last = pltpu.roll(g_first, width // 2, 1), pltpu.roll(v_last, width // 2, 1)
    for i, (middle, first, last) in enumerate(
        ((g_middle, g_first, g_last), (v_middle, v_first, v_last))
    ):
        first = jnp.where(low, first, 0.0)
        last = jnp.where(low, 0.0, last)
        for part, out in enumerate((to_below, own, to_above)):
            at = slice(part * c, (part + 1) * c)
            to = slice(i * c, (i + 1) * c)
            out[to] = middle[at]
            out[to, :width] = middle[at, :width] + first[at]
            out[to, cells - width :] = middle[at, cells - width :] + last[at]


def add_planes(own, below, above, out, grad_input):
    total = own[...] + below[...] + above[...]
    c = total.shape[0] // 2
    split_rows(total[c:], out)
    split_rows(total[:c], grad_input)


def split_rows(value, out):
    rows, z = out.shape[0], out.shape[2]
    lanes = value.shape[1]
    for r in range(rows):
        shifted = value if r == 0 else pltpu.roll(value, lanes - r * z, 1)
        out[r] = shifted[:, :z].astype(BF16)


def sum_pieces(scale, pieces, parts, out):
    rows = parts.shape[0] // pieces
    total = parts[:rows]
    for at in range(rows, rows * pieces, rows):
        total += parts[at : at + rows]
    total = total / scale
    for at in range(0, rows * pieces, rows):
        out[at : at + rows] = total


def join_halves(core, mine, other, out):
    half = mine.shape[1]
    is_low = core[0] == 0
    out[:, :half] = jnp.where(is_low, mine[...], other[...])
    out[:, half:] = jnp.where(is_low, other[...], mine[...])


def neighbours(value_up, value_down, axis):
    n = lax.axis_size(axis)
    up = [(i, i + 1) for i in range(n - 1)]
    down = [(i + 1, i) for i in range(n - 1)]
    return lax.ppermute(value_up, axis, up), lax.ppermute(value_down, axis, down)


def exchange_rows(value, axis):
    apart = value.reshape(value.shape[0], 1, value.shape[1])
    return lax.all_to_all(apart, axis, 0, 0, tiled=True).reshape(value.shape)


def body(volume, kernel, grad_out):
    _, rows, z, c = volume.shape
    taps, _, total = kernel.shape
    cells, lanes = rows * z, (rows + 2) * z
    groups = lax.axis_size("chan")
    pieces = lax.axis_size("x") * lax.axis_size("sy")
    devices = pieces * lax.axis_size("core")
    v = volume[0].transpose(0, 2, 1)
    g = grad_out[0].transpose(0, 2, 1)
    k = kernel.reshape(taps * c, total)
    core = lax.axis_index("core").reshape(1).astype(jnp.int32)
    work = 2 * taps * c * total * cells
    half_taps = (taps - taps // 2) * c
    weights = pl.cdiv(half_taps, 128) * 128
    width = 2 * cells + weights

    edge = jax.ShapeDtypeStruct((c, z), BF16)
    first, last, sends = pl.pallas_call(
        first_sends,
        out_shape=[edge, edge, jax.ShapeDtypeStruct((groups, c, width), BF16)],
        in_specs=[pl.BlockSpec(memory_space=pltpu.SMEM)]
        + [pl.BlockSpec(memory_space=pltpu.HBM)] * 3,
        out_specs=[pl.BlockSpec(memory_space=pltpu.VMEM)] * 3,
        scratch_shapes=[
            pltpu.VMEM((rows, c, z), BF16),
            pltpu.VMEM((rows, c, z), BF16),
            pltpu.VMEM((weights, total), BF16),
            pltpu.SemaphoreType.DMA((3,)),
        ],
        compiler_params=pltpu.CompilerParams(vmem_limit_bytes=60 * 2**20),
        cost_estimate=pl.CostEstimate(
            flops=0, bytes_accessed=groups * c * width * 4, transcendentals=0
        ),
    )(core, v, g, k)
    before, after = neighbours(last, first, "sy")
    received = lax.all_to_all(sends, "chan", 0, 0, axis_index_groups=[turn(groups)], tiled=True)
    (v_ring,) = call(volume_ring, [((c, lanes), BF16)], 0, v, before, after)
    v_below, v_above = neighbours(v_ring, v_ring, PLANE)

    def around(*refs):
        windows(z, *refs)

    (columns,) = call(around, [((taps * c, cells), BF16)], 0, v_below, v_ring, v_above)
    piece = (taps * c, total // 2)
    keep, send, k_mine = call(
        weight_terms,
        [(piece, F32), (piece, F32), ((total, half_taps), BF16)],
        work,
        core,
        columns,
        received,
    )
    swap = [(0, 1), (1, 0)]
    halves = keep + lax.ppermute(send, "core", swap)

    halves, k_mine, received = lax.optimization_barrier((halves, k_mine, received))
    parts = exchange_rows(halves, ("x", "sy"))
    k_other = lax.ppermute(k_mine, "core", swap)
    middle, ends = ((3 * c, cells), F32), ((3 * c, 2 * z), F32)

    def from_cotangent(*refs):
        spread_cotangent(z, *refs)

    def from_volume(*refs):
        spread_volume(z, *refs)

    g_middle, g_ends = call(from_cotangent, [middle, ends], work, received, k)
    (k_out,) = call(weights_by_output, [((taps * c, total), BF16)], 0, core, k_mine, k_other)
    v_middle, up, down = call(
        from_volume, [middle, ends, ends], work, received, k_out, g_ends
    )
    before, after = neighbours(up, down, "sy")
    parts, before, after = lax.optimization_barrier((parts, before, after))
    scale = math.sqrt(cells * devices)

    def reduce_pieces(*refs):
        sum_pieces(scale, pieces, *refs)

    (copies,) = call(reduce_pieces, [(piece, F32)], 0, parts)
    copies, before, after = lax.optimization_barrier((copies, before, after))
    mine = exchange_rows(copies, ("x", "sy"))
    own, to_below, to_above = call(
        add_ends, [((2 * c, cells), F32)] * 3, 0, g_middle, v_middle, before, after
    )
    below, above = neighbours(to_above, to_below, PLANE)
    result = ((rows, c, z), BF16)
    mine, below, above = lax.optimization_barrier((mine, below, above))
    out, grad_input = call(add_planes, [result, result], 0, own, below, above)
    other = lax.ppermute(mine, "core", swap)
    (grad_kernel,) = call(join_halves, [((taps * c, total), F32)], 0, core, mine, other)
    return (
        out.transpose(0, 2, 1)[None],
        grad_input.transpose(0, 2, 1)[None],
        grad_kernel.reshape(taps, c, total),
    )


def solution(mesh):
    cores = 2
    shape = (mesh.shape["chan"], mesh.shape["sx"] // cores, cores, mesh.shape["sy"])
    split = Mesh(mesh.devices.reshape(shape), ("chan", "x", "core", "sy"))
    cells = P(PLANE, "sy", None, "chan")
    weights = P(None, "chan", None)
    return jax.shard_map(
        body,
        mesh=split,
        in_specs=(cells, weights, cells),
        out_specs=(cells, cells, weights),
        check_vma=False,
    )
```

```python
import math

import jax
import jax.numpy as jnp
from jax import lax
from jax.experimental import pallas as pl
from jax.experimental.pallas import tpu as pltpu
from jax.sharding import Mesh
from jax.sharding import PartitionSpec as P

F32 = jnp.float32
BF16 = jnp.bfloat16
PLANE = ("x", "core")
TAPS = 27
PARAMS = pltpu.CompilerParams(vmem_limit_bytes=16 * 2**20)


def call(kernel, outs, flops, *args, scratch=()):
    moved = sum(a.size * a.dtype.itemsize for a in args)
    moved += sum(math.prod(s) * jnp.dtype(d).itemsize for s, d in outs)
    specs = [
        pl.BlockSpec(memory_space=pltpu.SMEM if a.dtype == jnp.int32 else pltpu.VMEM) for a in args
    ]
    return pl.pallas_call(
        kernel,
        out_shape=[jax.ShapeDtypeStruct(s, d) for s, d in outs],
        in_specs=specs,
        out_specs=[pl.BlockSpec(memory_space=pltpu.VMEM) for _ in outs],
        scratch_shapes=list(scratch),
        compiler_params=PARAMS,
        cost_estimate=pl.CostEstimate(flops=flops, bytes_accessed=moved, transcendentals=0),
    )(*args)


def first_sends(core, v, g, k, first, last, sends, v_own, g_own, k_own, sems):
    rows, c, z = g_own.shape
    cells = rows * z
    skip = TAPS // 2 * c
    held = k.shape[0] - skip
    moves = [
        pltpu.make_async_copy(v, v_own, sems.at[0]),
        pltpu.make_async_copy(g, g_own, sems.at[1]),
        pltpu.make_async_copy(
            k.at[pl.ds(pl.multiple_of(core[0] * skip, c), held)], k_own.at[pl.ds(0, held)], sems.at[2]
        ),
    ]
    for move in moves:
        move.start()
    k_own[held:] = jnp.zeros((k_own.shape[0] - held, k_own.shape[1]), BF16)
    moves[0].wait()
    first[...] = v_own[0]
    last[...] = v_own[rows - 1]
    v_flat = in_row([v_own[r] for r in range(rows)])
    moves[1].wait()
    g_flat = in_row([g_own[r] for r in range(rows)])
    moves[2].wait()
    turned = k_own[...].T
    for at, to in enumerate(turn(sends.shape[0])):
        sends[at, :, :cells] = g_flat
        sends[at, :, cells : 2 * cells] = v_flat
        sends[at, :, 2 * cells :] = turned[to * c : (to + 1) * c]


def turn(groups):
    return [(at + 5) % groups for at in range(groups)]


def by_chan(received, start, size):
    order = turn(received.shape[0])
    blocks = [received[order.index(i)][:, start : start + size] for i in range(len(order))]
    return jnp.concatenate(blocks, axis=0)


def in_row(parts):
    return jnp.concatenate(parts, axis=1)


def volume_ring(v, before, after, ring):
    ring[...] = in_row([v[r] for r in range(v.shape[0])] + [after[...], before[...]])


def weights_by_output(core, mine, other, k_out):
    c = k_out.shape[0] // TAPS
    groups = mine.shape[0] // c
    middle = TAPS // 2
    is_low = core[0] == 0
    a, b = mine[...], other[...]
    for tap in range(TAPS):
        half = jnp.where(is_low, a, b) if tap < middle else jnp.where(is_low, b, a)
        at = (tap if tap < middle else tap - middle) * c
        blocks = [half[i * c : (i + 1) * c, at : at + c] for i in range(groups)]
        k_out[tap * c : (tap + 1) * c] = in_row(blocks)


def in_line(shape, z, shift):
    at = lax.broadcasted_iota(jnp.int32, shape, 1) % z + shift
    return (at >= 0) & (at < z)


def windows(z, below, own, above, columns):
    c = own.shape[0]
    lanes = own.shape[1]
    cells = lanes - 2 * z
    planes = jnp.concatenate([below[...], own[...], above[...]], axis=0).astype(F32)
    for e in range(3):
        moved = planes if e == 1 else pltpu.roll(planes, (1 - e) % lanes, 1)
        if e != 1:
            moved = jnp.where(in_line(moved.shape, z, e - 1), moved, 0.0)
        for b in range(3):
            window = moved if b == 1 else pltpu.roll(moved, (z * (1 - b)) % lanes, 1)
            window = window[:, :cells].astype(BF16)
            for a in range(3):
                at = (9 * a + 3 * b + e) * c
                columns[at : at + c, :] = window[a * c : (a + 1) * c]


def weight_terms(core, columns, received, keep, send, k_mine):
    groups, c, _ = received.shape
    cells, total = columns.shape[1], groups * c
    g_own = by_chan(received, 0, cells)
    terms = lax.dot_general(
        columns[...], g_own, (((1,), (1,)), ((), ())), preferred_element_type=F32
    )
    half = total // 2
    low, high = terms[:, :half], terms[:, half:]
    is_low = core[0] == 0
    keep[...] = jnp.where(is_low, low, high)
    send[...] = jnp.where(is_low, high, low)
    k_mine[...] = by_chan(received, 2 * cells, k_mine.shape[1])


def spread(z, sign, own, k):
    lanes = own.shape[1] + 2 * z
    taps = k.shape[0] // 3
    c = taps // 9
    result = []
    for a in range(3)[:: -sign]:
        terms = jnp.dot(k[a * taps : (a + 1) * taps, :], own, preferred_element_type=F32)
        terms = jnp.concatenate([terms, jnp.zeros((taps, 2 * z), F32)], axis=1)
        plane = jnp.zeros((c, lanes), F32)
        for e in range(3):
            line = jnp.zeros((c, lanes), F32)
            for b in range(3):
                at = (3 * b + e) * c
                term = terms[at : at + c]
                line += term if b == 1 else pltpu.roll(term, (sign * z * (1 - b)) % lanes, 1)
            if e != 1:
                line = pltpu.roll(line, (sign * (1 - e)) % lanes, 1)
                line = jnp.where(in_line(line.shape, z, sign * (e - 1)), line, 0.0)
            plane += line
        result.append(plane)
    return result


def store_spread(planes, middle):
    c, cells = middle.shape[0] // 3, middle.shape[1]
    for i, plane in enumerate(planes):
        middle[i * c : (i + 1) * c] = plane[:, :cells]
    ends = jnp.concatenate([plane[:, cells:] for plane in planes], axis=0)
    z = ends.shape[1] // 2
    return ends, pltpu.roll(ends, z, 1)


def is_low_half(shape):
    return lax.broadcasted_iota(jnp.int32, shape, 1) < shape[1] // 2


def spread_cotangent(z, received, k, middle, ends):
    own = by_chan(received, 0, middle.shape[1])
    ends[...], _ = store_spread(spread(z, -1, own, k), middle)


def spread_volume(z, core, k_mine, k_other, received, g_ends, middle, up, down, k_out):
    weights_by_output(core, k_mine, k_other, k_out)
    cells = middle.shape[1]
    own = by_chan(received, cells, cells)
    ends, turned = store_spread(spread(z, 1, own, k_out), middle)
    low = is_low_half(ends.shape)
    up[...] = jnp.where(low, g_ends[...], turned)
    down[...] = jnp.where(low, pltpu.roll(g_ends[...], z, 1), ends)


def add_ends(g_middle, v_middle, before, after, own, to_below, to_above):
    rows, cells = g_middle.shape
    width = before.shape[1]
    c = rows // 3
    low = is_low_half(before.shape)
    g_first, v_last = before[...], after[...]
    v_first, g_last = pltpu.roll(g_first, width // 2, 1), pltpu.roll(v_last, width // 2, 1)
    for i, (middle, first, last) in enumerate(
        ((g_middle, g_first, g_last), (v_middle, v_first, v_last))
    ):
        first = jnp.where(low, first, 0.0)
        last = jnp.where(low, 0.0, last)
        for part, out in enumerate((to_below, own, to_above)):
            at = slice(part * c, (part + 1) * c)
            to = slice(i * c, (i + 1) * c)
            out[to] = middle[at]
            out[to, :width] = middle[at, :width] + first[at]
            out[to, cells - width :] = middle[at, cells - width :] + last[at]


def add_planes(own, below, above, out, grad_input):
    total = own[...] + below[...] + above[...]
    c = total.shape[0] // 2
    split_rows(total[c:], out)
    split_rows(total[:c], grad_input)


def split_rows(value, out):
    rows, z = out.shape[0], out.shape[2]
    lanes = value.shape[1]
    for r in range(rows):
        shifted = value if r == 0 else pltpu.roll(value, lanes - r * z, 1)
        out[r] = shifted[:, :z].astype(BF16)


def add_halves(keep, other, out):
    out[...] = keep[...] + other[...]


def sum_pieces(scale, pieces, parts, out):
    rows = parts.shape[0] // pieces
    total = parts[:rows]
    for at in range(rows, rows * pieces, rows):
        total += parts[at : at + rows]
    total = total / scale
    for at in range(0, rows * pieces, rows):
        out[at : at + rows] = total


def join_halves(core, mine, other, out):
    half = mine.shape[1]
    is_low = core[0] == 0
    out[:, :half] = jnp.where(is_low, mine[...], other[...])
    out[:, half:] = jnp.where(is_low, other[...], mine[...])


def neighbours(value_up, value_down, axis):
    n = lax.axis_size(axis)
    up = [(i, i + 1) for i in range(n - 1)]
    down = [(i + 1, i) for i in range(n - 1)]
    return lax.ppermute(value_up, axis, up), lax.ppermute(value_down, axis, down)


def exchange_rows(value, axis):
    apart = value.reshape(value.shape[0], 1, value.shape[1])
    return lax.all_to_all(apart, axis, 0, 0, tiled=True).reshape(value.shape)


def body(volume, kernel, grad_out):
    _, rows, z, c = volume.shape
    taps, _, total = kernel.shape
    cells, lanes = rows * z, (rows + 2) * z
    groups = lax.axis_size("chan")
    pieces = lax.axis_size("x") * lax.axis_size("sy")
    devices = pieces * lax.axis_size("core")
    v = volume[0].transpose(0, 2, 1)
    g = grad_out[0].transpose(0, 2, 1)
    k = kernel.reshape(taps * c, total)
    core = lax.axis_index("core").reshape(1).astype(jnp.int32)
    work = 2 * taps * c * total * cells
    half_taps = (taps - taps // 2) * c
    weights = pl.cdiv(half_taps, 128) * 128
    width = 2 * cells + weights

    edge = jax.ShapeDtypeStruct((c, z), BF16)
    first, last, sends = pl.pallas_call(
        first_sends,
        out_shape=[edge, edge, jax.ShapeDtypeStruct((groups, c, width), BF16)],
        in_specs=[pl.BlockSpec(memory_space=pltpu.SMEM)]
        + [pl.BlockSpec(memory_space=pltpu.HBM)] * 3,
        out_specs=[pl.BlockSpec(memory_space=pltpu.VMEM)] * 3,
        scratch_shapes=[
            pltpu.VMEM((rows, c, z), BF16),
            pltpu.VMEM((rows, c, z), BF16),
            pltpu.VMEM((weights, total), BF16),
            pltpu.SemaphoreType.DMA((3,)),
        ],
        compiler_params=pltpu.CompilerParams(vmem_limit_bytes=60 * 2**20),
        cost_estimate=pl.CostEstimate(
            flops=0, bytes_accessed=groups * c * width * 4, transcendentals=0
        ),
    )(core, v, g, k)
    before, after = neighbours(last, first, "sy")
    received = lax.all_to_all(sends, "chan", 0, 0, axis_index_groups=[turn(groups)], tiled=True)
    (v_ring,) = call(volume_ring, [((c, lanes), BF16)], 0, v, before, after)
    v_below, v_above = neighbours(v_ring, v_ring, PLANE)

    def around(*refs):
        windows(z, *refs)

    (columns,) = call(around, [((taps * c, cells), BF16)], 0, v_below, v_ring, v_above)
    piece = (taps * c, total // 2)
    keep, send, k_mine = call(
        weight_terms,
        [(piece, F32), (piece, F32), ((total, half_taps), BF16)],
        work,
        core,
        columns,
        received,
    )
    swap = [(0, 1), (1, 0)]
    (halves,) = call(add_halves, [(piece, F32)], 0, keep, lax.ppermute(send, "core", swap))

    halves, k_mine, received = lax.optimization_barrier((halves, k_mine, received))
    parts = exchange_rows(halves, ("x", "sy"))
    k_other = lax.ppermute(k_mine, "core", swap)
    middle, ends = ((3 * c, cells), F32), ((3 * c, 2 * z), F32)

    def from_cotangent(*refs):
        spread_cotangent(z, *refs)

    def from_volume(*refs):
        spread_volume(z, *refs)

    g_middle, g_ends = call(from_cotangent, [middle, ends], work, received, k)
    v_middle, up, down = call(
        from_volume,
        [middle, ends, ends],
        work,
        core,
        k_mine,
        k_other,
        received,
        g_ends,
        scratch=[pltpu.VMEM((taps * c, total), BF16)],
    )
    before, after = neighbours(up, down, "sy")
    parts, before, after = lax.optimization_barrier((parts, before, after))
    scale = math.sqrt(cells * devices)

    def reduce_pieces(*refs):
        sum_pieces(scale, pieces, *refs)

    (copies,) = call(reduce_pieces, [(piece, F32)], 0, parts)
    copies, before, after = lax.optimization_barrier((copies, before, after))
    mine = exchange_rows(copies, ("x", "sy"))
    own, to_below, to_above = call(
        add_ends, [((2 * c, cells), F32)] * 3, 0, g_middle, v_middle, before, after
    )
    below, above = neighbours(to_above, to_below, PLANE)
    result = ((rows, c, z), BF16)
    mine, below, above = lax.optimization_barrier((mine, below, above))
    out, grad_input = call(add_planes, [result, result], 0, own, below, above)
    other = lax.ppermute(mine, "core", swap)
    (grad_kernel,) = call(join_halves, [((taps * c, total), F32)], 0, core, mine, other)
    return (
        out.transpose(0, 2, 1)[None],
        grad_input.transpose(0, 2, 1)[None],
        grad_kernel.reshape(taps, c, total),
    )


def solution(mesh):
    cores = 2
    shape = (mesh.shape["chan"], mesh.shape["sx"] // cores, cores, mesh.shape["sy"])
    split = Mesh(mesh.devices.reshape(shape), ("chan", "x", "core", "sy"))
    cells = P(PLANE, "sy", None, "chan")
    weights = P(None, "chan", None)
    return jax.shard_map(
        body,
        mesh=split,
        in_specs=(cells, weights, cells),
        out_specs=(cells, cells, weights),
        check_vma=False,
    )
```

```python
import math

import jax
import jax.numpy as jnp
from jax import lax
from jax.experimental import pallas as pl
from jax.experimental.pallas import tpu as pltpu
from jax.sharding import Mesh
from jax.sharding import PartitionSpec as P

F32 = jnp.float32
BF16 = jnp.bfloat16
PLANE = ("x", "core")
TAPS = 27
PARAMS = pltpu.CompilerParams(vmem_limit_bytes=16 * 2**20)


def call(kernel, outs, flops, *args, scratch=()):
    moved = sum(a.size * a.dtype.itemsize for a in args)
    moved += sum(math.prod(s) * jnp.dtype(d).itemsize for s, d in outs)
    specs = [
        pl.BlockSpec(memory_space=pltpu.SMEM if a.dtype == jnp.int32 else pltpu.VMEM) for a in args
    ]
    return pl.pallas_call(
        kernel,
        out_shape=[jax.ShapeDtypeStruct(s, d) for s, d in outs],
        in_specs=specs,
        out_specs=[pl.BlockSpec(memory_space=pltpu.VMEM) for _ in outs],
        scratch_shapes=list(scratch),
        compiler_params=PARAMS,
        cost_estimate=pl.CostEstimate(flops=flops, bytes_accessed=moved, transcendentals=0),
    )(*args)


def first_sends(core, v, g, k, first, last, sends, v_own, g_own, k_own, sems):
    rows, c, z = g_own.shape
    cells = rows * z
    skip = TAPS // 2 * c
    held = k.shape[0] - skip
    moves = [
        pltpu.make_async_copy(v, v_own, sems.at[0]),
        pltpu.make_async_copy(g, g_own, sems.at[1]),
        pltpu.make_async_copy(
            k.at[pl.ds(pl.multiple_of(core[0] * skip, c), held)], k_own.at[pl.ds(0, held)], sems.at[2]
        ),
    ]
    for move in moves:
        move.start()
    k_own[held:] = jnp.zeros((k_own.shape[0] - held, k_own.shape[1]), BF16)
    moves[0].wait()
    first[...] = v_own[0]
    last[...] = v_own[rows - 1]
    v_flat = in_row([v_own[r] for r in range(rows)])
    moves[1].wait()
    g_flat = in_row([g_own[r] for r in range(rows)])
    moves[2].wait()
    turned = k_own[...].T
    for at, to in enumerate(turn(sends.shape[0])):
        sends[at, :, :cells] = g_flat
        sends[at, :, cells : 2 * cells] = v_flat
        sends[at, :, 2 * cells :] = turned[to * c : (to + 1) * c]


def turn(groups):
    return [(at + 5) % groups for at in range(groups)]


def by_chan(received, start, size):
    order = turn(received.shape[0])
    blocks = [received[order.index(i)][:, start : start + size] for i in range(len(order))]
    return jnp.concatenate(blocks, axis=0)


def in_row(parts):
    return jnp.concatenate(parts, axis=1)


def volume_ring(v, before, after, ring):
    ring[...] = in_row([v[r] for r in range(v.shape[0])] + [after[...], before[...]])


def weights_by_output(core, mine, other, k_out):
    c = k_out.shape[0] // TAPS
    groups = mine.shape[0] // c
    middle = TAPS // 2
    is_low = core[0] == 0
    a, b = mine[...], other[...]
    for tap in range(TAPS):
        half = jnp.where(is_low, a, b) if tap < middle else jnp.where(is_low, b, a)
        at = (tap if tap < middle else tap - middle) * c
        blocks = [half[i * c : (i + 1) * c, at : at + c] for i in range(groups)]
        k_out[tap * c : (tap + 1) * c] = in_row(blocks)


def in_line(shape, z, shift):
    at = lax.broadcasted_iota(jnp.int32, shape, 1) % z + shift
    return (at >= 0) & (at < z)


def windows(z, below, own, above, columns):
    c = own.shape[0]
    lanes = own.shape[1]
    cells = lanes - 2 * z
    planes = jnp.concatenate([below[...], own[...], above[...]], axis=0).astype(F32)
    for e in range(3):
        moved = planes if e == 1 else pltpu.roll(planes, (1 - e) % lanes, 1)
        if e != 1:
            moved = jnp.where(in_line(moved.shape, z, e - 1), moved, 0.0)
        for b in range(3):
            window = moved if b == 1 else pltpu.roll(moved, (z * (1 - b)) % lanes, 1)
            window = window[:, :cells].astype(BF16)
            for a in range(3):
                at = (9 * a + 3 * b + e) * c
                columns[at : at + c, :] = window[a * c : (a + 1) * c]


def weight_terms(core, columns, received, keep, send, k_mine):
    groups, c, _ = received.shape
    cells, total = columns.shape[1], groups * c
    g_own = by_chan(received, 0, cells)
    terms = lax.dot_general(
        columns[...], g_own, (((1,), (1,)), ((), ())), preferred_element_type=F32
    )
    half = total // 2
    low, high = terms[:, :half], terms[:, half:]
    is_low = core[0] == 0
    keep[...] = jnp.where(is_low, low, high)
    send[...] = jnp.where(is_low, high, low)
    k_mine[...] = by_chan(received, 2 * cells, k_mine.shape[1])


def spread(z, sign, own, k):
    lanes = own.shape[1] + 2 * z
    taps = k.shape[0] // 3
    c = taps // 9
    result = []
    for a in range(3)[:: -sign]:
        terms = jnp.dot(k[a * taps : (a + 1) * taps, :], own, preferred_element_type=F32)
        terms = jnp.concatenate([terms, jnp.zeros((taps, 2 * z), F32)], axis=1)
        plane = jnp.zeros((c, lanes), F32)
        for e in range(3):
            line = jnp.zeros((c, lanes), F32)
            for b in range(3):
                at = (3 * b + e) * c
                term = terms[at : at + c]
                line += term if b == 1 else pltpu.roll(term, (sign * z * (1 - b)) % lanes, 1)
            if e != 1:
                line = pltpu.roll(line, (sign * (1 - e)) % lanes, 1)
                line = jnp.where(in_line(line.shape, z, sign * (e - 1)), line, 0.0)
            plane += line
        result.append(plane)
    return result


def store_spread(planes, middle):
    c, cells = middle.shape[0] // 3, middle.shape[1]
    for i, plane in enumerate(planes):
        middle[i * c : (i + 1) * c] = plane[:, :cells]
    ends = jnp.concatenate([plane[:, cells:] for plane in planes], axis=0)
    z = ends.shape[1] // 2
    return ends, pltpu.roll(ends, z, 1)


def is_low_half(shape):
    return lax.broadcasted_iota(jnp.int32, shape, 1) < shape[1] // 2


def spread_cotangent(z, received, k, middle, ends):
    own = by_chan(received, 0, middle.shape[1])
    ends[...], _ = store_spread(spread(z, -1, own, k), middle)


def spread_volume(z, core, k_mine, k_other, received, g_ends, middle, up, down, k_out):
    weights_by_output(core, k_mine, k_other, k_out)
    cells = middle.shape[1]
    own = by_chan(received, cells, cells)
    ends, turned = store_spread(spread(z, 1, own, k_out), middle)
    low = is_low_half(ends.shape)
    up[...] = jnp.where(low, g_ends[...], turned)
    down[...] = jnp.where(low, pltpu.roll(g_ends[...], z, 1), ends)


def add_ends(g_middle, v_middle, before, after, own, to_below, to_above):
    rows, cells = g_middle.shape
    width = before.shape[1]
    c = rows // 3
    low = is_low_half(before.shape)
    g_first, v_last = before[...], after[...]
    v_first, g_last = pltpu.roll(g_first, width // 2, 1), pltpu.roll(v_last, width // 2, 1)
    for i, (middle, first, last) in enumerate(
        ((g_middle, g_first, g_last), (v_middle, v_first, v_last))
    ):
        first = jnp.where(low, first, 0.0)
        last = jnp.where(low, 0.0, last)
        for part, out in enumerate((to_below, own, to_above)):
            at = slice(part * c, (part + 1) * c)
            to = slice(i * c, (i + 1) * c)
            out[to] = middle[at]
            out[to, :width] = middle[at, :width] + first[at]
            out[to, cells - width :] = middle[at, cells - width :] + last[at]


def add_planes(own, below, above, out, grad_input):
    total = own[...] + below[...] + above[...]
    c = total.shape[0] // 2
    split_rows(total[c:], out)
    split_rows(total[:c], grad_input)


def split_rows(value, out):
    rows, z = out.shape[0], out.shape[2]
    lanes = value.shape[1]
    for r in range(rows):
        shifted = value if r == 0 else pltpu.roll(value, lanes - r * z, 1)
        out[r] = shifted[:, :z].astype(BF16)


def sum_pieces(scale, pieces, parts, out):
    rows = parts.shape[0] // pieces
    total = parts[:rows]
    for at in range(rows, rows * pieces, rows):
        total += parts[at : at + rows]
    total = total / scale
    for at in range(0, rows * pieces, rows):
        out[at : at + rows] = total


def join_halves(core, mine, other, out):
    half = mine.shape[1]
    is_low = core[0] == 0
    out[:, :half] = jnp.where(is_low, mine[...], other[...])
    out[:, half:] = jnp.where(is_low, other[...], mine[...])


def neighbours(value_up, value_down, axis):
    n = lax.axis_size(axis)
    up = [(i, i + 1) for i in range(n - 1)]
    down = [(i + 1, i) for i in range(n - 1)]
    return lax.ppermute(value_up, axis, up), lax.ppermute(value_down, axis, down)


def exchange_rows(value, axis):
    apart = value.reshape(value.shape[0], 1, value.shape[1])
    return lax.all_to_all(apart, axis, 0, 0, tiled=True).reshape(value.shape)


def body(volume, kernel, grad_out):
    _, rows, z, c = volume.shape
    taps, _, total = kernel.shape
    cells, lanes = rows * z, (rows + 2) * z
    groups = lax.axis_size("chan")
    pieces = lax.axis_size("x") * lax.axis_size("sy")
    devices = pieces * lax.axis_size("core")
    v = volume[0].transpose(0, 2, 1)
    g = grad_out[0].transpose(0, 2, 1)
    k = kernel.reshape(taps * c, total)
    core = lax.axis_index("core").reshape(1).astype(jnp.int32)
    work = 2 * taps * c * total * cells
    half_taps = (taps - taps // 2) * c
    weights = pl.cdiv(half_taps, 128) * 128
    width = 2 * cells + weights

    edge = jax.ShapeDtypeStruct((c, z), BF16)
    first, last, sends = pl.pallas_call(
        first_sends,
        out_shape=[edge, edge, jax.ShapeDtypeStruct((groups, c, width), BF16)],
        in_specs=[pl.BlockSpec(memory_space=pltpu.SMEM)]
        + [pl.BlockSpec(memory_space=pltpu.HBM)] * 3,
        out_specs=[pl.BlockSpec(memory_space=pltpu.VMEM)] * 3,
        scratch_shapes=[
            pltpu.VMEM((rows, c, z), BF16),
            pltpu.VMEM((rows, c, z), BF16),
            pltpu.VMEM((weights, total), BF16),
            pltpu.SemaphoreType.DMA((3,)),
        ],
        compiler_params=pltpu.CompilerParams(vmem_limit_bytes=60 * 2**20),
        cost_estimate=pl.CostEstimate(
            flops=0, bytes_accessed=groups * c * width * 4, transcendentals=0
        ),
    )(core, v, g, k)
    before, after = neighbours(last, first, "sy")
    received = lax.all_to_all(sends, "chan", 0, 0, axis_index_groups=[turn(groups)], tiled=True)
    (v_ring,) = call(volume_ring, [((c, lanes), BF16)], 0, v, before, after)
    v_below, v_above = neighbours(v_ring, v_ring, PLANE)

    def around(*refs):
        windows(z, *refs)

    (columns,) = call(around, [((taps * c, cells), BF16)], 0, v_below, v_ring, v_above)
    piece = (taps * c, total // 2)
    keep, send, k_mine = call(
        weight_terms,
        [(piece, F32), (piece, F32), ((total, half_taps), BF16)],
        work,
        core,
        columns,
        received,
    )
    swap = [(0, 1), (1, 0)]
    halves = keep + lax.ppermute(send, "core", swap)

    halves, k_mine, received = lax.optimization_barrier((halves, k_mine, received))
    parts = exchange_rows(halves, ("x", "sy"))
    k_other = lax.ppermute(k_mine, "core", swap)
    middle, ends = ((3 * c, cells), F32), ((3 * c, 2 * z), F32)

    def from_cotangent(*refs):
        spread_cotangent(z, *refs)

    def from_volume(*refs):
        spread_volume(z, *refs)

    g_middle, g_ends = call(from_cotangent, [middle, ends], work, received, k)
    v_middle, up, down = call(
        from_volume,
        [middle, ends, ends],
        work,
        core,
        k_mine,
        k_other,
        received,
        g_ends,
        scratch=[pltpu.VMEM((taps * c, total), BF16)],
    )
    before, after = neighbours(up, down, "sy")
    parts, before, after = lax.optimization_barrier((parts, before, after))
    scale = math.sqrt(cells * devices)

    def reduce_pieces(*refs):
        sum_pieces(scale, pieces, *refs)

    (copies,) = call(reduce_pieces, [(piece, F32)], 0, parts)
    copies, before, after = lax.optimization_barrier((copies, before, after))
    mine = exchange_rows(copies, ("x", "sy"))
    own, to_below, to_above = call(
        add_ends, [((2 * c, cells), F32)] * 3, 0, g_middle, v_middle, before, after
    )
    below, above = neighbours(to_above, to_below, PLANE)
    result = ((rows, c, z), BF16)
    mine, below, above = lax.optimization_barrier((mine, below, above))
    out, grad_input = call(add_planes, [result, result], 0, own, below, above)
    other = lax.ppermute(mine, "core", swap)
    (grad_kernel,) = call(join_halves, [((taps * c, total), F32)], 0, core, mine, other)
    return (
        out.transpose(0, 2, 1)[None],
        grad_input.transpose(0, 2, 1)[None],
        grad_kernel.reshape(taps, c, total),
    )


def solution(mesh):
    cores = 2
    shape = (mesh.shape["chan"], mesh.shape["sx"] // cores, cores, mesh.shape["sy"])
    split = Mesh(mesh.devices.reshape(shape), ("chan", "x", "core", "sy"))
    cells = P(PLANE, "sy", None, "chan")
    weights = P(None, "chan", None)
    return jax.shard_map(
        body,
        mesh=split,
        in_specs=(cells, weights, cells),
        out_specs=(cells, cells, weights),
        check_vma=False,
    )
```
